32 devices in a mesh: dp: 8 (over z, x), tensor: 4 (over y, core).
Axes of the slice: x: 2, y: 2, z: 4, core: 2. Of those that a mesh axis runs over, the one named last changes fastest.
Arguments:
- layer_input: bfloat16 [8192, 2048], P(('dp', 'tensor')), may hold values from -6 to 6
- query_weight: bfloat16 [2048, 2048], P('dp', 'tensor'), may hold values from -0.125 to 0.125
- key_weight: bfloat16 [2048, 2048], P('dp', 'tensor'), may hold values from -0.125 to 0.125
- value_weight: bfloat16 [2048, 2048], P('dp', 'tensor'), may hold values from -0.125 to 0.125
- out_weight: bfloat16 [2048, 2048], P('dp', 'tensor'), may hold values from -2 to 2
- gate_weight: bfloat16 [2048, 8192], P('dp', 'tensor'), may hold values from -0.125 to 0.125
- up_weight: bfloat16 [2048, 8192], P('dp', 'tensor'), may hold values from -0.125 to 0.125
- down_weight: bfloat16 [2048, 8192], P('dp', 'tensor'), may hold values from -0.0625 to 0.0625
- attention_gain: bfloat16 [2048], P('dp'), may hold values from 0.25 to 1.75
- feed_gain: bfloat16 [2048], P('dp'), may hold values from 0.25 to 1.75
- out_cotangent: bfloat16 [8192, 2048], P(('dp', 'tensor')), may hold values from -6 to 6
Outputs:
- layer_output: float32 [8192, 2048], P(('dp', 'tensor'))
- input_grad: float32 [8192, 2048], P(('dp', 'tensor'))
- query_grad: float32 [2048, 2048], P('dp', 'tensor')
- key_grad: float32 [2048, 2048], P('dp', 'tensor')
- value_grad: float32 [2048, 2048], P('dp', 'tensor')
- out_grad: float32 [2048, 2048], P('dp', 'tensor')
- gate_grad: float32 [2048, 8192], P('dp', 'tensor')
- up_grad: float32 [2048, 8192], P('dp', 'tensor')
- down_grad: float32 [2048, 8192], P('dp', 'tensor')
- attention_gain_grad: float32 [2048], P(('dp', 'tensor'))
- feed_gain_grad: float32 [2048], P(('dp', 'tensor'))
The draws below stay inside these ranges and needn't reach their ends.
All inputs are finite; a program needn't handle non-finite values.
Results may differ from the reference program's by a relative error of at most 0.019.
Values may be sent and summed in bfloat16 or wider, within the bound.
A program may use at most 256 MiB of HBM per device.

```python
import jax
import jax.numpy as jnp
from jax import lax

D = 2048
H = 32
HD = 64
FF = 8192
LEN = 1024
BLK = 256
TOKENS = 8192


def level_of(stream_key, shape, split, smallest, largest):
    def one(axis_at, shards_of):
        draws = jax.random.uniform(jax.random.fold_in(jax.random.fold_in(stream_key, 6), axis_at), (shards_of,), jnp.float32, smallest / len(split), largest / len(split))
        return jnp.repeat(jnp.exp(draws), shape[axis_at] // shards_of).reshape((-1,) + (1,) * (len(shape) - axis_at - 1))

    loudness = one(*split[0])
    for cut in split[1:]:
        loudness = loudness * one(*cut)
    return loudness


def gaussian(rng, extent, spread, most, shards=(), kind=jnp.bfloat16):
    loudness = level_of(rng, extent, shards, -0.22, 0.18) if shards else 1.0
    drawn = jax.random.normal(rng, extent, jnp.float32) * spread * loudness
    return jnp.minimum(jnp.maximum(drawn, -most), most).astype(kind)


def setup_inputs(seed: int = 0) -> dict:
    key_of = jax.random.split(jax.random.key(seed), 12)
    layer_input = gaussian(key_of[0], (TOKENS, D), 1.0, 6.0, ((0, 32),))
    query_weight = gaussian(key_of[1], (D, D), D ** -0.5, 0.125, ((0, 8), (1, 4)))
    key_weight = gaussian(key_of[2], (D, D), D ** -0.5, 0.125, ((0, 8), (1, 4)))
    value_weight = gaussian(key_of[3], (D, D), D ** -0.5, 0.125, ((0, 8), (1, 4)))
    out_weight = gaussian(key_of[4], (D, D), (4 * D // LEN) ** -0.5, 2.0, ((0, 8), (1, 4)))
    gate_weight = gaussian(key_of[5], (D, FF), D ** -0.5, 0.125, ((0, 8), (1, 4)))
    up_weight = gaussian(key_of[6], (D, FF), D ** -0.5, 0.125, ((0, 8), (1, 4)))
    down_weight = gaussian(key_of[7], (D, FF), FF ** -0.5, 0.0625, ((0, 8), (1, 4)))
    attention_gain = jnp.clip(1.0 + 0.15 * jax.random.normal(key_of[8], (D,), jnp.float32), 0.25, 1.75).astype(jnp.bfloat16)
    feed_gain = jnp.clip(1.0 + 0.15 * jax.random.normal(key_of[9], (D,), jnp.float32), 0.25, 1.75).astype(jnp.bfloat16)
    out_cotangent = gaussian(key_of[10], (TOKENS, D), 1.0, 6.0, ((0, 32),))
    return dict(layer_input=layer_input, query_weight=query_weight, key_weight=key_weight, value_weight=value_weight, out_weight=out_weight, gate_weight=gate_weight, up_weight=up_weight, down_weight=down_weight, attention_gain=attention_gain, feed_gain=feed_gain, out_cotangent=out_cotangent)


epsilon = 1e-05
rope_base = 130000.0
highest = lax.Precision.HIGHEST

@jax.custom_vjp
def low(v):
    return lax.optimization_barrier(v.astype(jnp.bfloat16)).astype(jnp.float32)

@jax.custom_vjp
def low_back(v):
    return v

def low_keep(v):
    return (low(v), None)

def low_pass(kept, grad):
    return (grad,)

def back_keep(v):
    return (v, None)

def back_low(kept, grad):
    return (low(grad),)
low.defvjp(low_keep, low_pass)
low_back.defvjp(back_keep, back_low)

def matmul(left_side, right_side):
    return jnp.dot(left_side, right_side, precision=highest, preferred_element_type=jnp.float32)

def matmul_t(left_side, right_side):
    return lax.dot_general(left_side, right_side, (((1,), (1,)), ((), ())), precision=highest, preferred_element_type=jnp.float32)

def rotate(tensor, places, direction):
    half_dim = HD // 2
    inverse = rope_base ** (-(jnp.arange(half_dim, dtype=jnp.float32) * 2.0 / HD))
    angles = places[:, None] * inverse[None, :]
    cosine = jnp.cos(angles)[:, None, :]
    sine_part = direction * jnp.sin(angles)[:, None, :]
    first_half = tensor[..., :half_dim]
    second_half = tensor[..., half_dim:]
    return jnp.concatenate([first_half * cosine - second_half * sine_part, second_half * cosine + first_half * sine_part], axis=-1)

def attend(queries, key_rows, val_rows):
    block_rows = min(512, LEN)
    block_count = LEN // block_rows
    scaling = HD ** (-0.5)
    key_group = jnp.arange(LEN) // BLK

    def one_block(block_pair):
        query_rows, offset = block_pair
        raw_scores = jnp.einsum('qhd,khd->hqk', query_rows, key_rows, precision=highest)
        scores = low_back(raw_scores) * scaling
        query_group = (offset + jnp.arange(block_rows)) // BLK
        visible = key_group[None, :] <= query_group[:, None]
        scores = jnp.where(visible[None], scores, -1e+30)
        row_top = lax.optimization_barrier(jnp.max(scores, axis=-1, keepdims=True))
        exp_scores = jnp.exp(scores - row_top)
        soft_weights = exp_scores / lax.optimization_barrier(jnp.sum(exp_scores, axis=-1, keepdims=True))
        return jnp.einsum('hqk,khd->qhd', low(soft_weights), val_rows, precision=highest)
    blocks = queries.reshape(block_count, block_rows, H, HD)
    offsets = jnp.arange(block_count) * block_rows
    result = lax.map(jax.checkpoint(one_block), (blocks, offsets))
    return result.reshape(LEN, H * HD)

def block_forward(inputs, query_weight, key_weight, value_weight, out_weight, gate_weight, up_weight, down_weight, attention_gain, feed_gain):
    places = jnp.arange(LEN).astype(jnp.float32)
    inv_one = lax.rsqrt(lax.optimization_barrier(jnp.mean(inputs * inputs, axis=-1, keepdims=True)) + epsilon)
    normed = low(inputs * inv_one * attention_gain)
    queries = low(rotate(low_back(matmul(normed, query_weight)).reshape(LEN, H, HD), places, 1.0))
    key_rows = low(rotate(low_back(matmul(normed, key_weight)).reshape(LEN, H, HD), places, 1.0))
    val_rows = low(low_back(matmul(normed, value_weight))).reshape(LEN, H, HD)
    attended = low(low_back(attend(queries, key_rows, val_rows)))
    hidden_state = inputs + low_back(matmul_t(attended, out_weight))
    inv_two = lax.rsqrt(lax.optimization_barrier(jnp.mean(hidden_state * hidden_state, axis=-1, keepdims=True)) + epsilon)
    normed_two = low(hidden_state * inv_two * feed_gain)
    gate_pre = low_back(matmul(normed_two, gate_weight))
    up_proj = low_back(matmul(normed_two, up_weight))
    activated = low(jax.nn.silu(gate_pre) * up_proj)
    return hidden_state + low_back(matmul_t(activated, down_weight))

def reference(layer_input, query_weight, key_weight, value_weight, out_weight, gate_weight, up_weight, down_weight, attention_gain, feed_gain, out_cotangent):
    weights = tuple((w_item.astype(jnp.float32) for w_item in (query_weight, key_weight, value_weight, out_weight, gate_weight, up_weight, down_weight, attention_gain, feed_gain)))
    seq_count = layer_input.shape[0] // LEN
    inputs = layer_input.astype(jnp.float32).reshape(seq_count, LEN, D)
    cotangents = out_cotangent.astype(jnp.float32).reshape(seq_count, LEN, D)

    def one_sequence(totals, seq_pair):
        seq_input, seq_cotangent = seq_pair
        result, pullback = jax.vjp(block_forward, seq_input, *weights)
        seq_grads = pullback(seq_cotangent)
        totals = tuple((total_item + grad_item for total_item, grad_item in zip(totals, seq_grads[1:])))
        return (totals, (result, seq_grads[0]))
    zero_grads = tuple((jnp.zeros(w_item.shape, jnp.float32) for w_item in weights))
    totals, (results, input_grads) = lax.scan(one_sequence, zero_grads, (inputs, cotangents))
    return (results.reshape(seq_count * LEN, D), input_grads.reshape(seq_count * LEN, D), totals[0], totals[1], totals[2], totals[3], totals[4], totals[5], totals[6], totals[7], totals[8])
```

```python
import jax
import jax.numpy as jnp
from jax import lax
from jax.experimental import pallas as pl
from jax.experimental.pallas import tpu as pltpu
from jax.sharding import Mesh, PartitionSpec as P

HD = 64
LEN = 1024
BLK = 256
PAIR = 2 * HD
CHUNKS = 2

epsilon = 1e-05
rope_base = 130000.0
group = ("i", "y", "c")
swap = [(0, 1), (1, 0)]


def contract(left_side, right_side, left_dim, right_dim):
    return lax.dot_general(
        left_side,
        right_side,
        (((left_dim,), (right_dim,)), ((), ())),
        preferred_element_type=jnp.float32,
    )


def token_gather(values):
    return lax.all_gather(values, group, axis=0, tiled=True)


def token_sum(partial_value):
    return lax.psum_scatter(
        partial_value.astype(jnp.bfloat16), group, scatter_dimension=0, tiled=True
    ).astype(jnp.float32)


def rope_tables():
    half_dim = HD // 2
    lanes = jnp.arange(PAIR)
    inverse = rope_base ** (-((lanes % half_dim).astype(jnp.float32) * 2.0 / HD))
    angles = jnp.arange(LEN, dtype=jnp.float32)[:, None] * inverse[None, :]
    sign = jnp.where(lanes % HD < half_dim, -1.0, 1.0)
    return jnp.cos(angles), jnp.sin(angles) * sign[None, :]


def turn(values, cosine, signed_sine):
    half_dim = HD // 2
    lanes = lax.broadcasted_iota(jnp.int32, values.shape, 1)
    other = jnp.where(
        lanes % HD < half_dim,
        pltpu.roll(values, PAIR - half_dim, 1),
        pltpu.roll(values, half_dim, 1),
    )
    return values * cosine + other * signed_sine


def head_parts(values):
    lanes = lax.broadcasted_iota(jnp.int32, values.shape, 1)
    empty = jnp.zeros_like(values)
    return [jnp.where(lanes // HD == head, values, empty) for head in range(2)]


def forward_kernel(
    query_ref, key_ref, value_ref, cos_ref, sin_ref, q_out, k_out, v_out, attended_out
):
    cosine, sine = cos_ref[...], sin_ref[...]
    queries = turn(query_ref[...], cosine, sine).astype(jnp.bfloat16)
    keys = turn(key_ref[...], cosine, sine).astype(jnp.bfloat16)
    values = value_ref[...].astype(jnp.bfloat16)
    q_out[...] = queries
    k_out[...] = keys
    v_out[...] = values
    value_parts = head_parts(values)
    scaling = HD**-0.5
    for block in range(LEN // BLK):
        rows = slice(block * BLK, (block + 1) * BLK)
        seen = (block + 1) * BLK
        total = None
        for head, query_part in enumerate(head_parts(queries[rows])):
            scores = contract(query_part, keys[:seen], 1, 1) * scaling
            top = jnp.max(scores, axis=-1, keepdims=True)
            powers = jnp.exp(scores - top)
            weights = powers / jnp.sum(powers, axis=-1, keepdims=True)
            term = contract(weights.astype(jnp.bfloat16), value_parts[head][:seen], 1, 0)
            total = term if total is None else total + term
        attended_out[rows, :] = total.astype(jnp.bfloat16)


def backward_kernel(
    query_ref, key_ref, value_ref, grad_ref, cos_ref, sin_ref, q_out, k_out, v_out, key_acc, value_acc
):
    keys, values = key_ref[...], value_ref[...]
    key_parts = head_parts(keys)
    scaling = HD**-0.5
    key_acc[...] = jnp.zeros_like(key_acc)
    value_acc[...] = jnp.zeros_like(value_acc)
    for block in range(LEN // BLK):
        rows = slice(block * BLK, (block + 1) * BLK)
        seen = (block + 1) * BLK
        query_parts = head_parts(query_ref[rows, :])
        grad_parts = head_parts(grad_ref[rows, :])
        query_delta = None
        for head in range(2):
            scores = contract(query_parts[head], keys[:seen], 1, 1) * scaling
            top = jnp.max(scores, axis=-1, keepdims=True)
            powers = jnp.exp(scores - top)
            weights = powers / jnp.sum(powers, axis=-1, keepdims=True)
            grad_probs = contract(grad_parts[head], values[:seen], 1, 1)
            row_dot = jnp.sum(weights * grad_probs, axis=-1, keepdims=True)
            grad_scores = (weights * (grad_probs - row_dot) * scaling).astype(jnp.bfloat16)
            term = contract(grad_scores, key_parts[head][:seen], 1, 0)
            query_delta = term if query_delta is None else query_delta + term
            key_acc[:seen, :] += contract(grad_scores, query_parts[head], 0, 0)
            value_acc[:seen, :] += contract(weights.astype(jnp.bfloat16), grad_parts[head], 0, 0)
        q_out[rows, :] = turn(query_delta, cos_ref[rows, :], -sin_ref[rows, :]).astype(jnp.bfloat16)
    k_out[...] = turn(key_acc[...], cos_ref[...], -sin_ref[...]).astype(jnp.bfloat16)
    v_out[...] = value_acc[...].astype(jnp.bfloat16)


def attention_cost(rows, width, products):
    return pl.CostEstimate(
        flops=2 * products * rows * LEN * width,
        bytes_accessed=8 * rows * width * 2,
        transcendentals=rows * LEN * width // HD,
    )


def attention_forward(mixed, tables):
    rows, width = mixed.shape[0], mixed.shape[1] // 3
    pairs = width // PAIR

    def part(which):
        return pl.BlockSpec((LEN, PAIR), lambda s, p: (s, which * pairs + p))

    whole = pl.BlockSpec((LEN, PAIR), lambda s, p: (0, 0))
    return pl.pallas_call(
        forward_kernel,
        grid=(rows // LEN, pairs),
        in_specs=[part(0), part(1), part(2), whole, whole],
        out_specs=[part(0)] * 4,
        out_shape=[jax.ShapeDtypeStruct((rows, width), jnp.bfloat16)] * 4,
        cost_estimate=attention_cost(rows, width, 2),
        name="attention_forward",
    )(mixed, mixed, mixed, *tables)


def attention_backward(queries, keys, values, grads, tables):
    rows, width = queries.shape
    part = pl.BlockSpec((LEN, PAIR), lambda s, p: (s, p))
    whole = pl.BlockSpec((LEN, PAIR), lambda s, p: (0, 0))
    return pl.pallas_call(
        backward_kernel,
        grid=(rows // LEN, width // PAIR),
        in_specs=[part] * 4 + [whole] * 2,
        out_specs=[part] * 3,
        out_shape=[jax.ShapeDtypeStruct((rows, width), jnp.bfloat16)] * 3,
        scratch_shapes=[pltpu.VMEM((LEN, PAIR), jnp.float32)] * 2,
        cost_estimate=attention_cost(rows, width, 5),
        name="attention_backward",
    )(queries, keys, values, grads, *tables)


def exchange_rows(weights, first, width):
    side = lax.axis_index("i")

    def columns(which):
        return jnp.concatenate(
            [
                lax.dynamic_slice_in_dim(w, which * (w.shape[1] // 2) + first, width, axis=1)
                for w in weights
            ],
            axis=1,
        )

    kept = columns(side)
    other = lax.ppermute(columns(1 - side), "i", swap)
    return jnp.where(
        side == 0, jnp.concatenate([kept, other]), jnp.concatenate([other, kept])
    )


def row_gather(values):
    return lax.all_gather(values, "o", axis=0, tiled=True)


def row_sum(partial_value):
    return lax.psum_scatter(partial_value, "o", scatter_dimension=0, tiled=True)


def exchange_columns(summed):
    side = lax.axis_index("i")
    rows = summed.shape[0] // 2
    kept = lax.dynamic_slice_in_dim(summed, side * rows, rows, axis=0)
    other = lax.ppermute(
        lax.dynamic_slice_in_dim(summed, (1 - side) * rows, rows, axis=0), "i", swap
    )
    return jnp.where(side == 0, kept, other), jnp.where(side == 0, other, kept)


def inverse_rms(values):
    return lax.rsqrt(jnp.mean(values * values, axis=-1, keepdims=True) + epsilon)


def per_device(
    layer_input,
    query_weight,
    key_weight,
    value_weight,
    out_weight,
    gate_weight,
    up_weight,
    down_weight,
    attention_gain,
    feed_gain,
    out_cotangent,
):
    head_width = query_weight.shape[1] // 2
    hidden = gate_weight.shape[1] // 2
    chunk = hidden // CHUNKS
    tables = rope_tables()

    attention_rows = exchange_rows(
        (query_weight, key_weight, value_weight, out_weight), 0, head_width
    )
    attention_full = row_gather(attention_rows)
    feed_full = [
        row_gather(exchange_rows((gate_weight, up_weight, down_weight), k * chunk, chunk))
        for k in range(CHUNKS)
    ]
    gains = lax.all_gather(
        jnp.stack([attention_gain, feed_gain]), ("o", "i"), axis=1, tiled=True
    ).astype(jnp.float32)
    gain_one, gain_two = gains[0], gains[1]

    inputs_all = token_gather(layer_input).astype(jnp.float32)
    normed = (inputs_all * inverse_rms(inputs_all) * gain_one).astype(jnp.bfloat16)
    cotangents = token_gather(out_cotangent)
    inputs = layer_input.astype(jnp.float32)
    inv_one = inverse_rms(inputs)
    normed_one = inputs * inv_one

    mixed = contract(normed, attention_full[:, : 3 * head_width], 1, 0)
    queries, keys, values, attended = attention_forward(mixed, tables)
    out_full = attention_full[:, 3 * head_width :]
    hidden_state = inputs + token_sum(contract(attended, out_full, 1, 1))
    inv_two = inverse_rms(hidden_state)
    normed_two_raw = hidden_state * inv_two
    normed_two = token_gather((normed_two_raw * gain_two).astype(jnp.bfloat16))

    output_part = None
    grad_part = None
    feed_grads = []
    for k in range(CHUNKS):
        gate_full = feed_full[k][:, :chunk]
        up_full = feed_full[k][:, chunk : 2 * chunk]
        down_full = feed_full[k][:, 2 * chunk :]
        gate_pre = contract(normed_two, gate_full, 1, 0)
        up_proj = contract(normed_two, up_full, 1, 0)
        grad_act = contract(cotangents, down_full, 1, 0)
        sigmoid_gate = jax.nn.sigmoid(gate_pre)
        silu_gate = gate_pre * sigmoid_gate
        activated = (silu_gate * up_proj).astype(jnp.bfloat16)
        gate_slope = sigmoid_gate * (1.0 + gate_pre * (1.0 - sigmoid_gate))
        grad_gate = (grad_act * up_proj * gate_slope).astype(jnp.bfloat16)
        grad_up = (grad_act * silu_gate).astype(jnp.bfloat16)
        grads = jnp.concatenate(
            [
                contract(normed_two, grad_gate, 0, 0).astype(jnp.bfloat16),
                contract(normed_two, grad_up, 0, 0).astype(jnp.bfloat16),
                contract(cotangents, activated, 0, 0).astype(jnp.bfloat16),
            ],
            axis=1,
        )
        feed_grads.append(exchange_columns(row_sum(grads)))
        out_term = contract(activated, down_full, 1, 1)
        grad_term = contract(grad_gate, gate_full, 1, 1) + contract(grad_up, up_full, 1, 1)
        output_part = out_term if output_part is None else output_part + out_term
        grad_part = grad_term if grad_part is None else grad_part + grad_term

    grad_normed_two = token_sum(grad_part)
    layer_output = hidden_state + token_sum(output_part)
    feed_gain_part = jnp.sum(grad_normed_two * normed_two_raw, axis=0)
    scaled_two = grad_normed_two * gain_two
    grad_hidden = out_cotangent.astype(jnp.float32) + inv_two * (
        scaled_two - normed_two_raw * jnp.mean(scaled_two * normed_two_raw, axis=-1, keepdims=True)
    )
    grad_rows = token_gather(grad_hidden.astype(jnp.bfloat16))
    grad_attended = contract(grad_rows, out_full, 1, 0).astype(jnp.bfloat16)
    grad_query, grad_key, grad_value = attention_backward(
        queries, keys, values, grad_attended, tables
    )
    grad_mixed = jnp.concatenate([grad_query, grad_key, grad_value], axis=1)
    attention_grads = jnp.concatenate(
        [
            contract(normed, grad_mixed, 0, 0).astype(jnp.bfloat16),
            contract(grad_rows, attended, 0, 0).astype(jnp.bfloat16),
        ],
        axis=1,
    )
    attention_halves = exchange_columns(row_sum(attention_grads))
    grad_normed = token_sum(contract(grad_mixed, attention_full[:, : 3 * head_width], 1, 1))
    attention_gain_part = jnp.sum(grad_normed * normed_one, axis=0)
    scaled_one = grad_normed * gain_one
    input_grad = grad_hidden + inv_one * (
        scaled_one - normed_one * jnp.mean(scaled_one * normed_one, axis=-1, keepdims=True)
    )

    def whole_rows(which):
        return jnp.concatenate(
            [
                half[:, which * head_width : (which + 1) * head_width]
                for half in attention_halves
            ],
            axis=1,
        ).astype(jnp.float32)

    def whole_feed_rows(which):
        return jnp.concatenate(
            [
                feed_grads[k][half][:, which * chunk : (which + 1) * chunk]
                for half in range(2)
                for k in range(CHUNKS)
            ],
            axis=1,
        ).astype(jnp.float32)

    gain_grads = [
        lax.psum_scatter(part, ("o", "i", "y", "c"), scatter_dimension=0, tiled=True)
        for part in (attention_gain_part, feed_gain_part)
    ]
    return (
        layer_output,
        input_grad,
        *[whole_rows(which) for which in range(4)],
        *[whole_feed_rows(which) for which in range(3)],
        *gain_grads,
    )


def solution(mesh):
    rows, columns = mesh.shape["dp"], mesh.shape["tensor"]
    fine = Mesh(
        mesh.devices.reshape(rows // 2, 2, columns // 2, 2), ("o", "i", "y", "c")
    )
    tokens = P(("o", "i", "y", "c"), None)
    weight = P(("o", "i"), ("y", "c"))
    gain = P(("o", "i"))
    return jax.shard_map(
        per_device,
        mesh=fine,
        in_specs=(tokens, *[weight] * 7, gain, gain, tokens),
        out_specs=(tokens, tokens, *[weight] * 7, P(("o", "i", "y", "c")), P(("o", "i", "y", "c"))),
        check_vma=False,
    )
```

```python
import jax
import jax.numpy as jnp
from jax import lax
from jax.experimental import pallas as pl
from jax.experimental.pallas import tpu as pltpu
from jax.sharding import Mesh, PartitionSpec as P

HD = 64
LEN = 1024
BLK = 256
PAIR = 2 * HD
CHUNKS = 2

epsilon = 1e-05
rope_base = 130000.0
group = ("i", "y", "c")
swap = [(0, 1), (1, 0)]


def contract(left_side, right_side, left_dim, right_dim):
    return lax.dot_general(
        left_side,
        right_side,
        (((left_dim,), (right_dim,)), ((), ())),
        preferred_element_type=jnp.float32,
    )


MESH = pl.DeviceIdType.MESH


def greet_partners():
    barrier = pltpu.get_barrier_semaphore()
    for axis in group:
        pl.semaphore_signal(
            barrier, inc=1, device_id={axis: 1 - lax.axis_index(axis)}, device_id_type=MESH
        )
    pl.semaphore_wait(barrier, 3)


def send_along(axis, source, target, semaphores, slot):
    return pltpu.make_async_remote_copy(
        src_ref=source,
        dst_ref=target,
        send_sem=semaphores.at[0, slot],
        recv_sem=semaphores.at[1, slot],
        device_id={axis: 1 - lax.axis_index(axis)},
        device_id_type=MESH,
    )


def first_row(flips, rows):
    i, y, c = [
        1 - lax.axis_index(axis) if axis in flips else lax.axis_index(axis) for axis in group
    ]
    return pl.multiple_of(((i * 2 + y) * 2 + c) * rows, rows)


def gather_kernel(count, *refs):
    sources, targets = refs[:count], refs[count : 2 * count]
    semaphores, own_semaphore = refs[2 * count :]
    rows = sources[0].shape[0]
    half = rows // 2
    greet_partners()

    def place(which, flips, part=None):
        start = first_row(flips, rows)
        if part is None:
            return targets[which].at[pl.ds(start, rows), :]
        return targets[which].at[pl.ds(start + part * half, half), :]

    started = []

    def send(which, axis, source, target, slot):
        copy = send_along(axis, source, target, semaphores.at[which], slot)
        copy.start()
        started.append(copy)
        return copy

    own, first = [], []
    for which in range(count):
        source = sources[which]
        own.append(
            pltpu.make_async_copy(source, place(which, ()), own_semaphore.at[which])
        )
        own[-1].start()
        top, bottom = source.at[pl.ds(0, half), :], source.at[pl.ds(half, half), :]
        first.append(
            [
                send(which, "i", top, place(which, (), 0), 0),
                send(which, "y", bottom, place(which, (), 1), 1),
                send(which, "i", bottom, place(which, (), 1), 2),
                send(which, "y", top, place(which, (), 0), 3),
                send(which, "c", source, place(which, ()), 4),
            ]
        )
    second = []
    for which in range(count):
        i_top, y_bottom, i_bottom, y_top, _ = first[which]
        i_top.wait_recv()
        onward = [send(which, "y", place(which, ("i",), 0), place(which, ("i",), 0), 5)]
        y_bottom.wait_recv()
        onward.append(send(which, "i", place(which, ("y",), 1), place(which, ("y",), 1), 6))
        i_bottom.wait_recv()
        onward.append(send(which, "c", place(which, ("i",)), place(which, ("i",)), 7))
        y_top.wait_recv()
        onward.append(send(which, "c", place(which, ("y",)), place(which, ("y",)), 8))
        second.append(onward)
    for which in range(count):
        top, bottom, i_side, y_side = second[which]
        top.wait_recv()
        across = ("i", "y")
        last = [send(which, "c", place(which, across, 0), place(which, across, 0), 9)]
        bottom.wait_recv()
        last.append(send(which, "c", place(which, across, 1), place(which, across, 1), 10))
        for copy in (first[which][4], i_side, y_side, *last):
            copy.wait_recv()
        own[which].wait()
    for copy in started:
        copy.wait_send()


def token_gather(*arrays):
    count = len(arrays)
    rows, width = arrays[0].shape
    gathered = pl.pallas_call(
        lambda *refs: gather_kernel(count, *refs),
        in_specs=[pl.BlockSpec(memory_space=pltpu.VMEM)] * count,
        out_specs=[pl.BlockSpec(memory_space=pl.ANY)] * count,
        out_shape=[jax.ShapeDtypeStruct((8 * rows, width), a.dtype) for a in arrays],
        scratch_shapes=[
            pltpu.SemaphoreType.DMA((count, 2, 11)),
            pltpu.SemaphoreType.DMA((count,)),
        ],
        compiler_params=pltpu.CompilerParams(collective_id=count, has_side_effects=True),
        cost_estimate=pl.CostEstimate(
            flops=0, bytes_accessed=100 * count * rows * width, transcendentals=0
        ),
        name=f"token_gather_{count}",
    )(*arrays)
    return gathered if count > 1 else gathered[0]


def scatter_kernel(windows, *refs):
    count = len(windows)
    lefts, rights, total = refs[:count], refs[count : 2 * count], refs[2 * count]
    (
        left_held,
        right_held,
        core_out,
        core_in,
        sums,
        first_i,
        first_y,
        second_i,
        second_y,
        left_semaphores,
        right_semaphores,
        semaphores,
    ) = refs[2 * count + 1 :]
    rows, width = total.shape
    half = rows // 2
    tile = 512
    relations = (("i", "y"), ("i",), ("y",), ())
    order = [(r, mine) for r in range(4) for mine in (False, True)]

    loads = []
    edge = 0
    for which, (left_start, right_start, depth) in enumerate(windows):
        copy = pltpu.make_async_copy(
            rights[which].at[:, pl.ds(right_start, depth)],
            right_held.at[:, pl.ds(edge, depth)],
            right_semaphores.at[which],
        )
        copy.start()
        loads.append(copy)
        edge += depth
    left_loads = []
    for step, (r, mine) in enumerate(order):
        flips = relations[r] if mine else relations[r] + ("c",)
        start = first_row(flips, rows)
        edge = 0
        row = []
        for which, (left_start, right_start, depth) in enumerate(windows):
            copy = pltpu.make_async_copy(
                lefts[which].at[pl.ds(start, rows), pl.ds(left_start, depth)],
                left_held.at[step, :, pl.ds(edge, depth)],
                left_semaphores.at[step, which],
            )
            copy.start()
            row.append(copy)
            edge += depth
        left_loads.append(row)
    greet_partners()
    for copy in loads:
        copy.wait()

    top, bottom = pl.ds(0, half), pl.ds(half, half)
    started = []

    def send(axis, source, target, slot):
        copy = send_along(axis, source, target, semaphores, slot)
        copy.start()
        started.append(copy)
        return copy

    core_copies, copies = [], {}
    for step, (r, mine) in enumerate(order):
        for copy in left_loads[step]:
            copy.wait()
        if mine:
            core_copies[r].wait_recv()

        def one_tile(t, carry):
            columns = pl.ds(pl.multiple_of(t * tile, tile), tile)
            part = contract(left_held[step], right_held[columns, :], 1, 1)
            if not mine:
                core_out[r, :, columns] = part.astype(jnp.bfloat16)
            elif r < 3:
                sums[r, :, columns] = (part + core_in[r, :, columns].astype(jnp.float32)).astype(
                    jnp.bfloat16
                )
            else:
                total[:, columns] = part + core_in[r, :, columns].astype(jnp.float32)
            return carry

        lax.fori_loop(0, width // tile, one_tile, 0)
        if not mine:
            core_copies.append(send("c", core_out.at[r], core_in.at[r], r))
        elif r == 0:
            copies["i1"] = send("i", sums.at[0, top, :], first_i.at[1], 4)
            copies["y1"] = send("y", sums.at[0, bottom, :], first_y.at[1], 5)
        elif r == 1:
            copies["i0"] = send("i", sums.at[1, top, :], first_i.at[0], 6)
        elif r == 2:
            copies["y0"] = send("y", sums.at[2, bottom, :], first_y.at[0], 7)
    copies["y1"].wait_recv()
    sums[1, bottom, :] = (
        sums[1, bottom, :].astype(jnp.float32) + first_y[1].astype(jnp.float32)
    ).astype(jnp.bfloat16)
    copies["i2"] = send("i", sums.at[1, bottom, :], second_i, 8)
    copies["i1"].wait_recv()
    sums[2, top, :] = (
        sums[2, top, :].astype(jnp.float32) + first_i[1].astype(jnp.float32)
    ).astype(jnp.bfloat16)
    copies["y2"] = send("y", sums.at[2, top, :], second_y, 9)
    copies["i0"].wait_recv()
    total[top, :] += first_i[0].astype(jnp.float32)
    copies["y0"].wait_recv()
    total[bottom, :] += first_y[0].astype(jnp.float32)
    copies["y2"].wait_recv()
    total[top, :] += second_y[...].astype(jnp.float32)
    copies["i2"].wait_recv()
    total[bottom, :] += second_i[...].astype(jnp.float32)
    for copy in started:
        copy.wait_send()


def product_sum(terms, name, number):
    rows, width = terms[0][0].shape[0] // 8, terms[0][2].shape[0]
    half = rows // 2
    count = len(terms)
    depth = sum(term[4] for term in terms)
    windows = [(term[1], term[3], term[4]) for term in terms]
    return pl.pallas_call(
        lambda *refs: scatter_kernel(windows, *refs),
        in_specs=[pl.BlockSpec(memory_space=pl.ANY)] * (2 * count),
        out_specs=pl.BlockSpec(memory_space=pltpu.VMEM),
        out_shape=jax.ShapeDtypeStruct((rows, width), jnp.float32),
        scratch_shapes=[
            pltpu.VMEM((8, rows, depth), jnp.bfloat16),
            pltpu.VMEM((width, depth), jnp.bfloat16),
            pltpu.VMEM((4, rows, width), jnp.bfloat16),
            pltpu.VMEM((4, rows, width), jnp.bfloat16),
            pltpu.VMEM((3, rows, width), jnp.bfloat16),
            pltpu.VMEM((2, half, width), jnp.bfloat16),
            pltpu.VMEM((2, half, width), jnp.bfloat16),
            pltpu.VMEM((half, width), jnp.bfloat16),
            pltpu.VMEM((half, width), jnp.bfloat16),
            pltpu.SemaphoreType.DMA((8, count)),
            pltpu.SemaphoreType.DMA((count,)),
            pltpu.SemaphoreType.DMA((2, 10)),
        ],
        compiler_params=pltpu.CompilerParams(collective_id=number, has_side_effects=True),
        cost_estimate=pl.CostEstimate(
            flops=16 * rows * depth * width, bytes_accessed=100 * rows * width, transcendentals=0
        ),
        name=name,
    )(*[term[0] for term in terms], *[term[2] for term in terms])


def rope_tables():
    half_dim = HD // 2
    lanes = jnp.arange(PAIR)
    inverse = rope_base ** (-((lanes % half_dim).astype(jnp.float32) * 2.0 / HD))
    angles = jnp.arange(LEN, dtype=jnp.float32)[:, None] * inverse[None, :]
    sign = jnp.where(lanes % HD < half_dim, -1.0, 1.0)
    return jnp.cos(angles), jnp.sin(angles) * sign[None, :]


def turn(values, cosine, signed_sine):
    half_dim = HD // 2
    lanes = lax.broadcasted_iota(jnp.int32, values.shape, 1)
    other = jnp.where(
        lanes % HD < half_dim,
        pltpu.roll(values, PAIR - half_dim, 1),
        pltpu.roll(values, half_dim, 1),
    )
    return values * cosine + other * signed_sine


def head_parts(values):
    lanes = lax.broadcasted_iota(jnp.int32, values.shape, 1)
    empty = jnp.zeros_like(values)
    return [jnp.where(lanes // HD == head, values, empty) for head in range(2)]


def forward_kernel(
    query_ref, key_ref, value_ref, cos_ref, sin_ref, q_out, k_out, v_out, attended_out
):
    cosine, sine = cos_ref[...], sin_ref[...]
    queries = turn(query_ref[...], cosine, sine).astype(jnp.bfloat16)
    keys = turn(key_ref[...], cosine, sine).astype(jnp.bfloat16)
    values = value_ref[...].astype(jnp.bfloat16)
    q_out[...] = queries
    k_out[...] = keys
    v_out[...] = values
    value_parts = head_parts(values)
    scaling = HD**-0.5
    for block in range(LEN // BLK):
        rows = slice(block * BLK, (block + 1) * BLK)
        seen = (block + 1) * BLK
        total = None
        for head, query_part in enumerate(head_parts(queries[rows])):
            scores = contract(query_part, keys[:seen], 1, 1) * scaling
            top = jnp.max(scores, axis=-1, keepdims=True)
            powers = jnp.exp(scores - top)
            weights = powers / jnp.sum(powers, axis=-1, keepdims=True)
            term = contract(weights.astype(jnp.bfloat16), value_parts[head][:seen], 1, 0)
            total = term if total is None else total + term
        attended_out[rows, :] = total.astype(jnp.bfloat16)


def backward_kernel(
    query_ref, key_ref, value_ref, grad_ref, cos_ref, sin_ref, q_out, k_out, v_out, key_acc, value_acc
):
    keys, values = key_ref[...], value_ref[...]
    key_parts = head_parts(keys)
    scaling = HD**-0.5
    key_acc[...] = jnp.zeros_like(key_acc)
    value_acc[...] = jnp.zeros_like(value_acc)
    for block in range(LEN // BLK):
        rows = slice(block * BLK, (block + 1) * BLK)
        seen = (block + 1) * BLK
        query_parts = head_parts(query_ref[rows, :])
        grad_parts = head_parts(grad_ref[rows, :])
        query_delta = None
        for head in range(2):
            scores = contract(query_parts[head], keys[:seen], 1, 1) * scaling
            top = jnp.max(scores, axis=-1, keepdims=True)
            powers = jnp.exp(scores - top)
            weights = powers / jnp.sum(powers, axis=-1, keepdims=True)
            grad_probs = contract(grad_parts[head], values[:seen], 1, 1)
            row_dot = jnp.sum(weights * grad_probs, axis=-1, keepdims=True)
            grad_scores = (weights * (grad_probs - row_dot) * scaling).astype(jnp.bfloat16)
            term = contract(grad_scores, key_parts[head][:seen], 1, 0)
            query_delta = term if query_delta is None else query_delta + term
            key_acc[:seen, :] += contract(grad_scores, query_parts[head], 0, 0)
            value_acc[:seen, :] += contract(weights.astype(jnp.bfloat16), grad_parts[head], 0, 0)
        q_out[rows, :] = turn(query_delta, cos_ref[rows, :], -sin_ref[rows, :]).astype(jnp.bfloat16)
    k_out[...] = turn(key_acc[...], cos_ref[...], -sin_ref[...]).astype(jnp.bfloat16)
    v_out[...] = value_acc[...].astype(jnp.bfloat16)


def attention_cost(rows, width, products):
    return pl.CostEstimate(
        flops=2 * products * rows * LEN * width,
        bytes_accessed=8 * rows * width * 2,
        transcendentals=rows * LEN * width // HD,
    )


def attention_forward(mixed, tables):
    rows, width = mixed.shape[0], mixed.shape[1] // 3
    pairs = width // PAIR

    def part(which):
        return pl.BlockSpec((LEN, PAIR), lambda s, p: (s, which * pairs + p))

    whole = pl.BlockSpec((LEN, PAIR), lambda s, p: (0, 0))
    return pl.pallas_call(
        forward_kernel,
        grid=(rows // LEN, pairs),
        in_specs=[part(0), part(1), part(2), whole, whole],
        out_specs=[part(0)] * 4,
        out_shape=[jax.ShapeDtypeStruct((rows, width), jnp.bfloat16)] * 4,
        cost_estimate=attention_cost(rows, width, 2),
        name="attention_forward",
    )(mixed, mixed, mixed, *tables)


def attention_backward(queries, keys, values, grads, tables):
    rows, width = queries.shape
    part = pl.BlockSpec((LEN, PAIR), lambda s, p: (s, p))
    whole = pl.BlockSpec((LEN, PAIR), lambda s, p: (0, 0))
    return pl.pallas_call(
        backward_kernel,
        grid=(rows // LEN, width // PAIR),
        in_specs=[part] * 4 + [whole] * 2,
        out_specs=[part] * 3,
        out_shape=[jax.ShapeDtypeStruct((rows, width), jnp.bfloat16)] * 3,
        scratch_shapes=[pltpu.VMEM((LEN, PAIR), jnp.float32)] * 2,
        cost_estimate=attention_cost(rows, width, 5),
        name="attention_backward",
    )(queries, keys, values, grads, *tables)


def exchange_rows(weights, first, width):
    side = lax.axis_index("i")

    def columns(which):
        return jnp.concatenate(
            [
                lax.dynamic_slice_in_dim(w, which * (w.shape[1] // 2) + first, width, axis=1)
                for w in weights
            ],
            axis=1,
        )

    kept = columns(side)
    other = lax.ppermute(columns(1 - side), "i", swap)
    return jnp.where(
        side == 0, jnp.concatenate([kept, other]), jnp.concatenate([other, kept])
    )


def row_gather(values):
    return lax.all_gather(values, "o", axis=0, tiled=True)


def row_sum(partial_value):
    return lax.psum_scatter(partial_value, "o", scatter_dimension=0, tiled=True)


def exchange_columns(summed):
    side = lax.axis_index("i")
    rows = summed.shape[0] // 2
    kept = lax.dynamic_slice_in_dim(summed, side * rows, rows, axis=0)
    other = lax.ppermute(
        lax.dynamic_slice_in_dim(summed, (1 - side) * rows, rows, axis=0), "i", swap
    )
    return jnp.where(side == 0, kept, other), jnp.where(side == 0, other, kept)


def inverse_rms(values):
    return lax.rsqrt(jnp.mean(values * values, axis=-1, keepdims=True) + epsilon)


def per_device(
    layer_input,
    query_weight,
    key_weight,
    value_weight,
    out_weight,
    gate_weight,
    up_weight,
    down_weight,
    attention_gain,
    feed_gain,
    out_cotangent,
):
    head_width = query_weight.shape[1] // 2
    hidden = gate_weight.shape[1] // 2
    chunk = hidden // CHUNKS
    tables = rope_tables()

    attention_rows = exchange_rows(
        (query_weight, key_weight, value_weight, out_weight), 0, head_width
    )
    attention_full = row_gather(attention_rows)
    feed_full = [
        row_gather(exchange_rows((gate_weight, up_weight, down_weight), k * chunk, chunk))
        for k in range(CHUNKS)
    ]
    gains = lax.all_gather(
        jnp.stack([attention_gain, feed_gain]), ("o", "i"), axis=1, tiled=True
    ).astype(jnp.float32)
    gain_one, gain_two = gains[0], gains[1]

    inputs_all, cotangents = token_gather(layer_input, out_cotangent)
    inputs_all = inputs_all.astype(jnp.float32)
    normed = (inputs_all * inverse_rms(inputs_all) * gain_one).astype(jnp.bfloat16)
    inputs = layer_input.astype(jnp.float32)
    inv_one = inverse_rms(inputs)
    normed_one = inputs * inv_one

    mixed = contract(normed, attention_full[:, : 3 * head_width], 1, 0)
    queries, keys, values, attended = attention_forward(mixed, tables)
    out_full = attention_full[:, 3 * head_width :]
    hidden_state = inputs + product_sum(
        [(attended, 0, attention_full, 3 * head_width, head_width)], "attention_output", 3
    )
    inv_two = inverse_rms(hidden_state)
    normed_two_raw = hidden_state * inv_two
    normed_two = token_gather((normed_two_raw * gain_two).astype(jnp.bfloat16))

    output_terms, grad_terms, feed_grads = [], [], []
    for k in range(CHUNKS):
        gate_full = feed_full[k][:, :chunk]
        up_full = feed_full[k][:, chunk : 2 * chunk]
        down_full = feed_full[k][:, 2 * chunk :]
        gate_pre = contract(normed_two, gate_full, 1, 0)
        up_proj = contract(normed_two, up_full, 1, 0)
        grad_act = contract(cotangents, down_full, 1, 0)
        sigmoid_gate = jax.nn.sigmoid(gate_pre)
        silu_gate = gate_pre * sigmoid_gate
        activated = (silu_gate * up_proj).astype(jnp.bfloat16)
        gate_slope = sigmoid_gate * (1.0 + gate_pre * (1.0 - sigmoid_gate))
        grad_gate = (grad_act * up_proj * gate_slope).astype(jnp.bfloat16)
        grad_up = (grad_act * silu_gate).astype(jnp.bfloat16)
        grads = jnp.concatenate(
            [
                contract(normed_two, grad_gate, 0, 0).astype(jnp.bfloat16),
                contract(normed_two, grad_up, 0, 0).astype(jnp.bfloat16),
                contract(cotangents, activated, 0, 0).astype(jnp.bfloat16),
            ],
            axis=1,
        )
        feed_grads.append(exchange_columns(row_sum(grads)))
        output_terms.append((activated, 0, feed_full[k], 2 * chunk, chunk))
        grad_terms.append((grad_gate, 0, feed_full[k], 0, chunk))
        grad_terms.append((grad_up, 0, feed_full[k], chunk, chunk))

    grad_normed_two = product_sum(grad_terms, "feed_gradient", 4)
    layer_output = hidden_state + product_sum(output_terms, "feed_output", 5)
    feed_gain_part = jnp.sum(grad_normed_two * normed_two_raw, axis=0)
    scaled_two = grad_normed_two * gain_two
    grad_hidden = out_cotangent.astype(jnp.float32) + inv_two * (
        scaled_two - normed_two_raw * jnp.mean(scaled_two * normed_two_raw, axis=-1, keepdims=True)
    )
    grad_rows = token_gather(grad_hidden.astype(jnp.bfloat16))
    grad_attended = contract(grad_rows, out_full, 1, 0).astype(jnp.bfloat16)
    grad_query, grad_key, grad_value = attention_backward(
        queries, keys, values, grad_attended, tables
    )
    grad_mixed = jnp.concatenate([grad_query, grad_key, grad_value], axis=1)
    attention_grads = jnp.concatenate(
        [
            contract(normed, grad_mixed, 0, 0).astype(jnp.bfloat16),
            contract(grad_rows, attended, 0, 0).astype(jnp.bfloat16),
        ],
        axis=1,
    )
    attention_halves = exchange_columns(row_sum(attention_grads))
    grad_normed = product_sum(
        [(grad_mixed, 0, attention_full, 0, 3 * head_width)], "attention_gradient", 6
    )
    attention_gain_part = jnp.sum(grad_normed * normed_one, axis=0)
    scaled_one = grad_normed * gain_one
    input_grad = grad_hidden + inv_one * (
        scaled_one - normed_one * jnp.mean(scaled_one * normed_one, axis=-1, keepdims=True)
    )

    def whole_rows(which):
        return jnp.concatenate(
            [
                half[:, which * head_width : (which + 1) * head_width]
                for half in attention_halves
            ],
            axis=1,
        ).astype(jnp.float32)

    def whole_feed_rows(which):
        return jnp.concatenate(
            [
                feed_grads[k][half][:, which * chunk : (which + 1) * chunk]
                for half in range(2)
                for k in range(CHUNKS)
            ],
            axis=1,
        ).astype(jnp.float32)

    gain_grads = [
        lax.psum_scatter(part, ("o", "i", "y", "c"), scatter_dimension=0, tiled=True)
        for part in (attention_gain_part, feed_gain_part)
    ]
    return (
        layer_output,
        input_grad,
        *[whole_rows(which) for which in range(4)],
        *[whole_feed_rows(which) for which in range(3)],
        *gain_grads,
    )


def solution(mesh):
    rows, columns = mesh.shape["dp"], mesh.shape["tensor"]
    fine = Mesh(
        mesh.devices.reshape(rows // 2, 2, columns // 2, 2), ("o", "i", "y", "c")
    )
    tokens = P(("o", "i", "y", "c"), None)
    weight = P(("o", "i"), ("y", "c"))
    gain = P(("o", "i"))
    return jax.shard_map(
        per_device,
        mesh=fine,
        in_specs=(tokens, *[weight] * 7, gain, gain, tokens),
        out_specs=(tokens, tokens, *[weight] * 7, P(("o", "i", "y", "c")), P(("o", "i", "y", "c"))),
        check_vma=False,
    )
```

```python
import jax
import jax.numpy as jnp
from jax import lax
from jax.experimental import pallas as pl
from jax.experimental.pallas import tpu as pltpu
from jax.sharding import Mesh, PartitionSpec as P

HD = 64
LEN = 1024
BLK = 256
PAIR = 2 * HD
CHUNKS = 2

epsilon = 1e-05
rope_base = 130000.0
group = ("i", "y", "c")
swap = [(0, 1), (1, 0)]


def contract(left_side, right_side, left_dim, right_dim):
    return lax.dot_general(
        left_side,
        right_side,
        (((left_dim,), (right_dim,)), ((), ())),
        preferred_element_type=jnp.float32,
    )


MESH = pl.DeviceIdType.MESH


def row_partner(shift, outer):
    return {"o": lax.rem(lax.axis_index("o") + shift, outer)}


def greet_partners(outer=1):
    barrier = pltpu.get_barrier_semaphore()
    partners = [{axis: 1 - lax.axis_index(axis)} for axis in group]
    partners += [row_partner(shift, outer) for shift in range(1, outer)]
    for partner in partners:
        pl.semaphore_signal(barrier, inc=1, device_id=partner, device_id_type=MESH)
    pl.semaphore_wait(barrier, len(partners))


def send_along(axis, source, target, semaphores, slot):
    return pltpu.make_async_remote_copy(
        src_ref=source,
        dst_ref=target,
        send_sem=semaphores.at[0, slot],
        recv_sem=semaphores.at[1, slot],
        device_id={axis: 1 - lax.axis_index(axis)},
        device_id_type=MESH,
    )


def first_row(flips, rows):
    i, y, c = [
        1 - lax.axis_index(axis) if axis in flips else lax.axis_index(axis) for axis in group
    ]
    return pl.multiple_of(((i * 2 + y) * 2 + c) * rows, rows)


def gather_kernel(outer, *refs):
    source, target, semaphores, own_semaphore = refs
    rows = source.shape[0]
    half = rows // 2
    greet_partners(outer)

    def place(flips, part=None):
        start = first_row(flips, rows)
        if part is None:
            return target.at[pl.ds(start, rows), :]
        return target.at[pl.ds(start + part * half, half), :]

    started = []

    def send(axis, source, target, slot):
        copy = send_along(axis, source, target, semaphores, slot)
        copy.start()
        started.append(copy)
        return copy

    own = pltpu.make_async_copy(source, place(()), own_semaphore)
    own.start()
    top, bottom = source.at[pl.ds(0, half), :], source.at[pl.ds(half, half), :]
    i_top = send("i", top, place((), 0), 0)
    y_bottom = send("y", bottom, place((), 1), 1)
    i_bottom = send("i", bottom, place((), 1), 2)
    y_top = send("y", top, place((), 0), 3)
    core = [send("c", source, place(()), 4)]
    i_top.wait_recv()
    across_top = send("y", place(("i",), 0), place(("i",), 0), 5)
    y_bottom.wait_recv()
    across_bottom = send("i", place(("y",), 1), place(("y",), 1), 6)
    i_bottom.wait_recv()
    core.append(send("c", place(("i",)), place(("i",)), 7))
    y_top.wait_recv()
    core.append(send("c", place(("y",)), place(("y",)), 8))
    across_top.wait_recv()
    core.append(send("c", place(("i", "y"), 0), place(("i", "y"), 0), 9))
    across_bottom.wait_recv()
    core.append(send("c", place(("i", "y"), 1), place(("i", "y"), 1), 10))
    for copy in core:
        copy.wait_recv()
    own.wait()
    for copy in started:
        copy.wait_send()


def opening_kernel(outer, token_ref, gain_ref, token_out, gain_out, *scratch):
    semaphores, own_semaphore, side_semaphores, row_semaphores = scratch
    me, side = lax.axis_index("o"), lax.axis_index("i")

    gather_kernel(outer, token_ref, token_out, semaphores, own_semaphore)
    gain_out[me * 2 + side] = gain_ref[...]
    along = send_along("i", gain_ref, gain_out.at[me * 2 + side], side_semaphores, 0)
    along.start()
    started = [along]

    def send_rows(source, slot, first):
        for shift in range(1, outer):
            copy = pltpu.make_async_remote_copy(
                src_ref=source,
                dst_ref=gain_out.at[slot],
                send_sem=row_semaphores.at[0, first, shift],
                recv_sem=row_semaphores.at[1, first, shift],
                device_id=row_partner(shift, outer),
                device_id_type=MESH,
            )
            copy.start()
            started.append(copy)

    send_rows(gain_ref, me * 2 + side, 0)
    along.wait_recv()
    send_rows(gain_out.at[me * 2 + 1 - side], me * 2 + 1 - side, 1)
    for copy in started[1:]:
        copy.wait_recv()
    for copy in started:
        copy.wait_send()


def opening_gather(array, gains, outer):
    rows, width = array.shape
    padded = jnp.pad(gains, ((0, 16 - gains.shape[0]), (0, 0)))
    vmem, hbm = pl.BlockSpec(memory_space=pltpu.VMEM), pl.BlockSpec(memory_space=pl.ANY)
    gathered, gain_rows = pl.pallas_call(
        lambda *refs: opening_kernel(outer, *refs),
        in_specs=[vmem] * 2,
        out_specs=[hbm, vmem],
        out_shape=[
            jax.ShapeDtypeStruct((8 * rows, width), array.dtype),
            jax.ShapeDtypeStruct((2 * outer, *padded.shape), gains.dtype),
        ],
        scratch_shapes=[
            pltpu.SemaphoreType.DMA((2, 11)),
            pltpu.SemaphoreType.DMA(()),
            pltpu.SemaphoreType.DMA((2, 1)),
            pltpu.SemaphoreType.DMA((2, 2, max(outer, 2))),
        ],
        compiler_params=pltpu.CompilerParams(collective_id=2, has_side_effects=True),
        cost_estimate=pl.CostEstimate(
            flops=0, bytes_accessed=200 * rows * width, transcendentals=0
        ),
        name="opening_gather",
    )(array, padded)
    return gathered, [gain_rows[:, which].reshape(-1) for which in range(2)]


def token_gather(array):
    rows, width = array.shape
    return pl.pallas_call(
        lambda *refs: gather_kernel(1, *refs),
        in_specs=[pl.BlockSpec(memory_space=pltpu.VMEM)],
        out_specs=pl.BlockSpec(memory_space=pl.ANY),
        out_shape=jax.ShapeDtypeStruct((8 * rows, width), array.dtype),
        scratch_shapes=[pltpu.SemaphoreType.DMA((2, 11)), pltpu.SemaphoreType.DMA(())],
        compiler_params=pltpu.CompilerParams(collective_id=1, has_side_effects=True),
        cost_estimate=pl.CostEstimate(
            flops=0, bytes_accessed=200 * rows * width, transcendentals=0
        ),
        name="token_gather",
    )(array)


def total_kernel(outer, part_ref, total_ref, held, stages, semaphores, row_semaphores):
    greet_partners(outer)
    started = []
    source, value = part_ref, part_ref[...]
    for step, axis in enumerate(group):
        copy = send_along(axis, source, held.at[step], semaphores, step)
        copy.start()
        started.append(copy)
        copy.wait_recv()
        value = value + held[step]
        stages[step] = value
        source = stages.at[step]
    copies = []
    for shift in range(1, outer):
        copy = pltpu.make_async_remote_copy(
            src_ref=source,
            dst_ref=held.at[2 + shift],
            send_sem=row_semaphores.at[0, shift],
            recv_sem=row_semaphores.at[1, shift],
            device_id=row_partner(shift, outer),
            device_id_type=MESH,
        )
        copy.start()
        copies.append(copy)
    for shift, copy in enumerate(copies):
        copy.wait_recv()
        value = value + held[3 + shift]
    total_ref[...] = value
    for copy in started + copies:
        copy.wait_send()


def sum_everywhere(part, outer):
    folded = part.reshape(-1, 128)
    spec = pl.BlockSpec(memory_space=pltpu.VMEM)
    return pl.pallas_call(
        lambda *refs: total_kernel(outer, *refs),
        in_specs=[spec],
        out_specs=spec,
        out_shape=jax.ShapeDtypeStruct(folded.shape, jnp.float32),
        scratch_shapes=[
            pltpu.VMEM((2 + outer, *folded.shape), jnp.float32),
            pltpu.VMEM((3, *folded.shape), jnp.float32),
            pltpu.SemaphoreType.DMA((2, 3)),
            pltpu.SemaphoreType.DMA((2, max(outer, 2))),
        ],
        compiler_params=pltpu.CompilerParams(collective_id=7, has_side_effects=True),
        name="sum_everywhere",
    )(folded).reshape(part.shape)


def scatter_kernel(windows, *refs):
    count = len(windows)
    lefts, rights, total = refs[:count], refs[count : 2 * count], refs[2 * count]
    (
        left_held,
        right_held,
        core_out,
        core_in,
        sums,
        first_i,
        first_y,
        second_i,
        second_y,
        left_semaphores,
        right_semaphores,
        semaphores,
    ) = refs[2 * count + 1 :]
    rows, width = total.shape
    half = rows // 2
    tile = 512
    relations = (("i", "y"), ("i",), ("y",), ())
    order = [(r, mine) for r in range(4) for mine in (False, True)]

    loads = []
    edge = 0
    for which, (left_start, right_start, depth) in enumerate(windows):
        copy = pltpu.make_async_copy(
            rights[which].at[:, pl.ds(right_start, depth)],
            right_held.at[:, pl.ds(edge, depth)],
            right_semaphores.at[which],
        )
        copy.start()
        loads.append(copy)
        edge += depth
    left_loads = []
    for step, (r, mine) in enumerate(order):
        flips = relations[r] if mine else relations[r] + ("c",)
        start = first_row(flips, rows)
        edge = 0
        row = []
        for which, (left_start, right_start, depth) in enumerate(windows):
            copy = pltpu.make_async_copy(
                lefts[which].at[pl.ds(start, rows), pl.ds(left_start, depth)],
                left_held.at[step, :, pl.ds(edge, depth)],
                left_semaphores.at[step, which],
            )
            copy.start()
            row.append(copy)
            edge += depth
        left_loads.append(row)
    greet_partners()
    for copy in loads:
        copy.wait()

    top, bottom = pl.ds(0, half), pl.ds(half, half)
    started = []

    def send(axis, source, target, slot):
        copy = send_along(axis, source, target, semaphores, slot)
        copy.start()
        started.append(copy)
        return copy

    core_copies, copies = [], {}
    for step, (r, mine) in enumerate(order):
        for copy in left_loads[step]:
            copy.wait()
        if mine:
            core_copies[r].wait_recv()

        def one_tile(t, carry):
            columns = pl.ds(pl.multiple_of(t * tile, tile), tile)
            part = contract(left_held[step], right_held[columns, :], 1, 1)
            if not mine:
                core_out[r, :, columns] = part.astype(jnp.bfloat16)
            elif r < 3:
                sums[r, :, columns] = (part + core_in[r, :, columns].astype(jnp.float32)).astype(
                    jnp.bfloat16
                )
            else:
                total[:, columns] = part + core_in[r, :, columns].astype(jnp.float32)
            return carry

        lax.fori_loop(0, width // tile, one_tile, 0)
        if not mine:
            core_copies.append(send("c", core_out.at[r], core_in.at[r], r))
        elif r == 0:
            copies["i1"] = send("i", sums.at[0, top, :], first_i.at[1], 4)
            copies["y1"] = send("y", sums.at[0, bottom, :], first_y.at[1], 5)
        elif r == 1:
            copies["i0"] = send("i", sums.at[1, top, :], first_i.at[0], 6)
        elif r == 2:
            copies["y0"] = send("y", sums.at[2, bottom, :], first_y.at[0], 7)
            copies["y1"].wait_recv()
            sums[1, bottom, :] = (
                sums[1, bottom, :].astype(jnp.float32) + first_y[1].astype(jnp.float32)
            ).astype(jnp.bfloat16)
            copies["i2"] = send("i", sums.at[1, bottom, :], second_i, 8)
            copies["i1"].wait_recv()
            sums[2, top, :] = (
                sums[2, top, :].astype(jnp.float32) + first_i[1].astype(jnp.float32)
            ).astype(jnp.bfloat16)
            copies["y2"] = send("y", sums.at[2, top, :], second_y, 9)
    copies["i0"].wait_recv()
    total[top, :] += first_i[0].astype(jnp.float32)
    copies["y0"].wait_recv()
    total[bottom, :] += first_y[0].astype(jnp.float32)
    copies["y2"].wait_recv()
    total[top, :] += second_y[...].astype(jnp.float32)
    copies["i2"].wait_recv()
    total[bottom, :] += second_i[...].astype(jnp.float32)
    for copy in started:
        copy.wait_send()


def product_sum(terms, number):
    rows, width = terms[0][0].shape[0] // 8, terms[0][2].shape[0]
    half = rows // 2
    count = len(terms)
    depth = sum(term[4] for term in terms)
    windows = [(term[1], term[3], term[4]) for term in terms]
    return pl.pallas_call(
        lambda *refs: scatter_kernel(windows, *refs),
        in_specs=[pl.BlockSpec(memory_space=pl.ANY)] * (2 * count),
        out_specs=pl.BlockSpec(memory_space=pltpu.VMEM),
        out_shape=jax.ShapeDtypeStruct((rows, width), jnp.float32),
        scratch_shapes=[
            pltpu.VMEM((8, rows, depth), jnp.bfloat16),
            pltpu.VMEM((width, depth), jnp.bfloat16),
            pltpu.VMEM((4, rows, width), jnp.bfloat16),
            pltpu.VMEM((4, rows, width), jnp.bfloat16),
            pltpu.VMEM((3, rows, width), jnp.bfloat16),
            pltpu.VMEM((2, half, width), jnp.bfloat16),
            pltpu.VMEM((2, half, width), jnp.bfloat16),
            pltpu.VMEM((half, width), jnp.bfloat16),
            pltpu.VMEM((half, width), jnp.bfloat16),
            pltpu.SemaphoreType.DMA((8, count)),
            pltpu.SemaphoreType.DMA((count,)),
            pltpu.SemaphoreType.DMA((2, 10)),
        ],
        compiler_params=pltpu.CompilerParams(collective_id=number, has_side_effects=True),
        cost_estimate=pl.CostEstimate(
            flops=16 * rows * depth * width, bytes_accessed=100 * rows * width, transcendentals=0
        ),
    )(*[term[0] for term in terms], *[term[2] for term in terms])


def rope_tables():
    half_dim = HD // 2
    lanes = jnp.arange(PAIR)
    inverse = rope_base ** (-((lanes % half_dim).astype(jnp.float32) * 2.0 / HD))
    angles = jnp.arange(LEN, dtype=jnp.float32)[:, None] * inverse[None, :]
    sign = jnp.where(lanes % HD < half_dim, -1.0, 1.0)
    return jnp.cos(angles), jnp.sin(angles) * sign[None, :]


def turn(values, cosine, signed_sine):
    half_dim = HD // 2
    lanes = lax.broadcasted_iota(jnp.int32, values.shape, 1)
    other = jnp.where(
        lanes % HD < half_dim,
        pltpu.roll(values, PAIR - half_dim, 1),
        pltpu.roll(values, half_dim, 1),
    )
    return values * cosine + other * signed_sine


def head_parts(values):
    lanes = lax.broadcasted_iota(jnp.int32, values.shape, 1)
    empty = jnp.zeros_like(values)
    return [jnp.where(lanes // HD == head, values, empty) for head in range(2)]


def forward_kernel(
    query_ref, key_ref, value_ref, cos_ref, sin_ref, q_out, k_out, v_out, attended_out
):
    cosine, sine = cos_ref[...], sin_ref[...]
    queries = turn(query_ref[...], cosine, sine).astype(jnp.bfloat16)
    keys = turn(key_ref[...], cosine, sine).astype(jnp.bfloat16)
    values = value_ref[...].astype(jnp.bfloat16)
    q_out[...] = queries
    k_out[...] = keys
    v_out[...] = values
    value_parts = head_parts(values)
    scaling = HD**-0.5
    for block in range(LEN // BLK):
        rows = slice(block * BLK, (block + 1) * BLK)
        seen = (block + 1) * BLK
        total = None
        for head, query_part in enumerate(head_parts(queries[rows])):
            scores = contract(query_part, keys[:seen], 1, 1) * scaling
            top = jnp.max(scores, axis=-1, keepdims=True)
            powers = jnp.exp(scores - top)
            weights = powers / jnp.sum(powers, axis=-1, keepdims=True)
            term = contract(weights.astype(jnp.bfloat16), value_parts[head][:seen], 1, 0)
            total = term if total is None else total + term
        attended_out[rows, :] = total.astype(jnp.bfloat16)


def backward_kernel(
    query_ref, key_ref, value_ref, grad_ref, cos_ref, sin_ref, q_out, k_out, v_out, key_acc, value_acc
):
    keys, values = key_ref[...], value_ref[...]
    key_parts = head_parts(keys)
    scaling = HD**-0.5
    key_acc[...] = jnp.zeros_like(key_acc)
    value_acc[...] = jnp.zeros_like(value_acc)
    for block in range(LEN // BLK):
        rows = slice(block * BLK, (block + 1) * BLK)
        seen = (block + 1) * BLK
        query_parts = head_parts(query_ref[rows, :])
        grad_parts = head_parts(grad_ref[rows, :])
        query_delta = None
        for head in range(2):
            scores = contract(query_parts[head], keys[:seen], 1, 1) * scaling
            top = jnp.max(scores, axis=-1, keepdims=True)
            powers = jnp.exp(scores - top)
            weights = powers / jnp.sum(powers, axis=-1, keepdims=True)
            grad_probs = contract(grad_parts[head], values[:seen], 1, 1)
            row_dot = jnp.sum(weights * grad_probs, axis=-1, keepdims=True)
            grad_scores = (weights * (grad_probs - row_dot) * scaling).astype(jnp.bfloat16)
            term = contract(grad_scores, key_parts[head][:seen], 1, 0)
            query_delta = term if query_delta is None else query_delta + term
            key_acc[:seen, :] += contract(grad_scores, query_parts[head], 0, 0)
            value_acc[:seen, :] += contract(weights.astype(jnp.bfloat16), grad_parts[head], 0, 0)
        q_out[rows, :] = turn(query_delta, cos_ref[rows, :], -sin_ref[rows, :]).astype(jnp.bfloat16)
    k_out[...] = turn(key_acc[...], cos_ref[...], -sin_ref[...]).astype(jnp.bfloat16)
    v_out[...] = value_acc[...].astype(jnp.bfloat16)


def attention_cost(rows, width, products):
    return pl.CostEstimate(
        flops=2 * products * rows * LEN * width,
        bytes_accessed=8 * rows * width * 2,
        transcendentals=rows * LEN * width // HD,
    )


def attention_forward(mixed, tables):
    rows, width = mixed.shape[0], mixed.shape[1] // 3
    pairs = width // PAIR

    def part(which):
        return pl.BlockSpec((LEN, PAIR), lambda s, p: (s, which * pairs + p))

    whole = pl.BlockSpec((LEN, PAIR), lambda s, p: (0, 0))
    return pl.pallas_call(
        forward_kernel,
        grid=(rows // LEN, pairs),
        in_specs=[part(0), part(1), part(2), whole, whole],
        out_specs=[part(0)] * 4,
        out_shape=[jax.ShapeDtypeStruct((rows, width), jnp.bfloat16)] * 4,
        cost_estimate=attention_cost(rows, width, 2),
        name="attention_forward",
    )(mixed, mixed, mixed, *tables)


def attention_backward(queries, keys, values, grads, tables):
    rows, width = queries.shape
    part = pl.BlockSpec((LEN, PAIR), lambda s, p: (s, p))
    whole = pl.BlockSpec((LEN, PAIR), lambda s, p: (0, 0))
    return pl.pallas_call(
        backward_kernel,
        grid=(rows // LEN, width // PAIR),
        in_specs=[part] * 4 + [whole] * 2,
        out_specs=[part] * 3,
        out_shape=[jax.ShapeDtypeStruct((rows, width), jnp.bfloat16)] * 3,
        scratch_shapes=[pltpu.VMEM((LEN, PAIR), jnp.float32)] * 2,
        cost_estimate=attention_cost(rows, width, 5),
        name="attention_backward",
    )(queries, keys, values, grads, *tables)


def feed_kernel(normed_ref, cotangent_ref, weight_ref, out_ref):
    chunk = out_ref.shape[1] // 3
    gate, up, down = [slice(which * chunk, (which + 1) * chunk) for which in range(3)]
    gate_pre = contract(normed_ref[...], weight_ref[:, gate], 1, 0)
    up_proj = contract(normed_ref[...], weight_ref[:, up], 1, 0)
    grad_act = contract(cotangent_ref[...], weight_ref[:, down], 1, 0)
    sigmoid_gate = jax.nn.sigmoid(gate_pre)
    silu_gate = gate_pre * sigmoid_gate
    gate_slope = sigmoid_gate * (1.0 + gate_pre * (1.0 - sigmoid_gate))
    out_ref[:, gate] = (grad_act * up_proj * gate_slope).astype(jnp.bfloat16)
    out_ref[:, up] = (grad_act * silu_gate).astype(jnp.bfloat16)
    out_ref[:, down] = (silu_gate * up_proj).astype(jnp.bfloat16)


def feed_units(normed, cotangents, weights):
    (rows, width), columns = normed.shape, weights.shape[1]
    tile = 256
    tokens = pl.BlockSpec((tile, width), lambda t: (t, 0))
    return pl.pallas_call(
        feed_kernel,
        grid=(rows // tile,),
        in_specs=[tokens, tokens, pl.BlockSpec((width, columns), lambda t: (0, 0))],
        out_specs=pl.BlockSpec((tile, columns), lambda t: (t, 0)),
        out_shape=jax.ShapeDtypeStruct((rows, columns), jnp.bfloat16),
        cost_estimate=pl.CostEstimate(
            flops=2 * rows * width * columns,
            bytes_accessed=2 * (2 * rows * width + width * columns + rows * columns),
            transcendentals=rows * columns // 3,
        ),
        name="feed_units",
    )(normed, cotangents, weights)


def weight_grads(terms):
    rows, width = terms[0][0].shape
    tile = 256
    operands, specs, plan = [], [], []
    for left, rights in terms:
        operands.append(left)
        specs.append(pl.BlockSpec((rows, tile), lambda t: (0, t)))
        for right, start, columns in rights:
            operands.append(right)
            specs.append(
                pl.BlockSpec((rows, columns), lambda t, block=start // columns: (0, block))
            )
        plan.append([columns for _, _, columns in rights])
    total = sum(sum(widths) for widths in plan)

    def kernel(*refs):
        edge, at = 0, 0
        for widths in plan:
            left = refs[at][...]
            at += 1
            for columns in widths:
                refs[-1][:, edge : edge + columns] = contract(left, refs[at][...], 0, 0).astype(
                    jnp.bfloat16
                )
                edge += columns
                at += 1

    return pl.pallas_call(
        kernel,
        grid=(width // tile,),
        in_specs=specs,
        out_specs=pl.BlockSpec((tile, total), lambda t: (t, 0)),
        out_shape=jax.ShapeDtypeStruct((width, total), jnp.bfloat16),
        cost_estimate=pl.CostEstimate(
            flops=2 * rows * width * total,
            bytes_accessed=2 * (2 * rows * width + width * total + rows * total),
            transcendentals=0,
        ),
    )(*operands)


def exchange_rows(weights, first, width):
    side = lax.axis_index("i")

    def columns(half):
        start = [half * (w.shape[1] // 2) + first for w in weights]
        return jnp.concatenate([w[:, a : a + width] for w, a in zip(weights, start)], axis=1)

    low, high = columns(0), columns(1)
    kept = jnp.where(side == 0, low, high)
    other = lax.ppermute(jnp.where(side == 0, high, low), "i", swap)
    return jnp.concatenate(
        [jnp.where(side == 0, kept, other), jnp.where(side == 0, other, kept)]
    )


def row_gather(values):
    return lax.all_gather(values, "o", axis=0, tiled=True)


def row_sum(partial_value):
    return lax.psum_scatter(partial_value, "o", scatter_dimension=0, tiled=True)


def exchange_columns(summed):
    side = lax.axis_index("i")
    rows = summed.shape[0] // 2
    kept = lax.dynamic_slice_in_dim(summed, side * rows, rows, axis=0)
    other = lax.ppermute(
        lax.dynamic_slice_in_dim(summed, (1 - side) * rows, rows, axis=0), "i", swap
    )
    return jnp.where(side == 0, kept, other), jnp.where(side == 0, other, kept)


def inverse_rms(values):
    return lax.rsqrt(jnp.mean(values * values, axis=-1, keepdims=True) + epsilon)


def per_device(
    layer_input,
    query_weight,
    key_weight,
    value_weight,
    out_weight,
    gate_weight,
    up_weight,
    down_weight,
    attention_gain,
    feed_gain,
    out_cotangent,
):
    head_width = query_weight.shape[1] // 2
    hidden = gate_weight.shape[1] // 2
    chunk = hidden // CHUNKS
    tables = rope_tables()
    outer = lax.axis_size("o")

    attention_rows = exchange_rows(
        (query_weight, key_weight, value_weight, out_weight), 0, head_width
    )
    attention_full = row_gather(attention_rows)
    feed_full = []
    for k in range(CHUNKS):
        feed_rows = exchange_rows((gate_weight, up_weight, down_weight), k * chunk, chunk)
        feed_full.append(row_gather(feed_rows))
    inputs_all, gains = opening_gather(layer_input, jnp.stack([attention_gain, feed_gain]), outer)
    inputs_all, late = lax.optimization_barrier((inputs_all, out_cotangent))
    cotangents = token_gather(late)
    gain_one, gain_two = [g.astype(jnp.float32) for g in gains]
    inputs_all = inputs_all.astype(jnp.float32)
    normed = (inputs_all * inverse_rms(inputs_all) * gain_one).astype(jnp.bfloat16)
    inputs = layer_input.astype(jnp.float32)
    inv_one = inverse_rms(inputs)
    normed_one = inputs * inv_one

    mixed = contract(normed, attention_full[:, : 3 * head_width], 1, 0)
    queries, keys, values, attended = attention_forward(mixed, tables)
    out_full = attention_full[:, 3 * head_width :]
    hidden_state = inputs + product_sum(
        [(attended, 0, attention_full, 3 * head_width, head_width)], 3
    )
    inv_two = inverse_rms(hidden_state)
    normed_two_raw = hidden_state * inv_two
    normed_two = token_gather((normed_two_raw * gain_two).astype(jnp.bfloat16))

    output_terms, grad_terms, feed_grads = [], [], []
    for k in range(CHUNKS):
        units = feed_units(normed_two, cotangents, feed_full[k])
        grads = weight_grads(
            [
                (normed_two, [(units, 0, 2 * chunk)]),
                (cotangents, [(units, 2 * chunk, chunk)]),
            ],
        )
        units, grads, normed_two, cotangents = lax.optimization_barrier(
            (units, grads, normed_two, cotangents)
        )
        summed = row_sum(grads)
        feed_grads.append(exchange_columns(summed))
        grad_terms.append((units, 0, feed_full[k], 0, 2 * chunk))
        output_terms.append((units, 2 * chunk, feed_full[k], 2 * chunk, chunk))

    grad_normed_two = product_sum(grad_terms, 4)
    feed_gain_part = jnp.sum(grad_normed_two * normed_two_raw, axis=0)
    scaled_two = grad_normed_two * gain_two
    grad_hidden = out_cotangent.astype(jnp.float32) + inv_two * (
        scaled_two - normed_two_raw * jnp.mean(scaled_two * normed_two_raw, axis=-1, keepdims=True)
    )
    grad_rows = token_gather(grad_hidden.astype(jnp.bfloat16))
    grad_attended = contract(grad_rows, out_full, 1, 0).astype(jnp.bfloat16)
    grad_query, grad_key, grad_value = attention_backward(
        queries, keys, values, grad_attended, tables
    )
    attention_grads = weight_grads(
        [
            (normed, [(g, 0, head_width) for g in (grad_query, grad_key, grad_value)]),
            (grad_rows, [(attended, 0, head_width)]),
        ],
    )
    attention_grads, grad_query = lax.optimization_barrier((attention_grads, grad_query))
    attention_summed = row_sum(attention_grads)
    attention_halves = exchange_columns(attention_summed)
    grad_normed = product_sum(
        [
            (g, 0, attention_full, which * head_width, head_width)
            for which, g in enumerate((grad_query, grad_key, grad_value))
        ],
        6,
    )
    last_units, grad_normed = lax.optimization_barrier((output_terms[-1][0], grad_normed))
    output_terms[-1] = (last_units, *output_terms[-1][1:])
    layer_output = hidden_state + product_sum(output_terms, 5)
    attention_gain_part = jnp.sum(grad_normed * normed_one, axis=0)
    scaled_one = grad_normed * gain_one
    input_grad = grad_hidden + inv_one * (
        scaled_one - normed_one * jnp.mean(scaled_one * normed_one, axis=-1, keepdims=True)
    )

    def whole_rows(which):
        return jnp.concatenate(
            [
                half[:, which * head_width : (which + 1) * head_width]
                for half in attention_halves
            ],
            axis=1,
        ).astype(jnp.float32)

    def whole_feed_rows(which):
        return jnp.concatenate(
            [
                feed_grads[k][half][:, which * chunk : (which + 1) * chunk]
                for half in range(2)
                for k in range(CHUNKS)
            ],
            axis=1,
        ).astype(jnp.float32)

    gain_sums = sum_everywhere(jnp.stack([attention_gain_part, feed_gain_part]), outer)
    device = lax.axis_index("o")
    for axis in group:
        device = device * 2 + lax.axis_index(axis)
    share = attention_gain.shape[0] // 4
    gain_grads = [
        lax.dynamic_slice_in_dim(gain_sums[which], device * share, share) for which in range(2)
    ]
    return (
        layer_output,
        input_grad,
        *[whole_rows(which) for which in range(4)],
        *[whole_feed_rows(which) for which in range(3)],
        *gain_grads,
    )


def solution(mesh):
    rows, columns = mesh.shape["dp"], mesh.shape["tensor"]
    fine = Mesh(
        mesh.devices.reshape(rows // 2, 2, columns // 2, 2), ("o", "i", "y", "c")
    )
    tokens = P(("o", "i", "y", "c"), None)
    weight = P(("o", "i"), ("y", "c"))
    gain = P(("o", "i"))

    return jax.shard_map(
        per_device,
        mesh=fine,
        in_specs=(tokens, *[weight] * 7, gain, gain, tokens),
        out_specs=(tokens, tokens, *[weight] * 7, P(("o", "i", "y", "c")), P(("o", "i", "y", "c"))),
        check_vma=False,
    )
```

```python
import jax
import jax.numpy as jnp
from jax import lax
from jax.experimental import pallas as pl
from jax.experimental.pallas import tpu as pltpu
from jax.sharding import Mesh, PartitionSpec as P

HD = 64
LEN = 1024
BLK = 256
PAIR = 2 * HD
CHUNKS = 2

epsilon = 1e-05
rope_base = 130000.0
group = ("i", "y", "c")
swap = [(0, 1), (1, 0)]


def contract(left_side, right_side, left_dim, right_dim):
    return lax.dot_general(
        left_side,
        right_side,
        (((left_dim,), (right_dim,)), ((), ())),
        preferred_element_type=jnp.float32,
    )


MESH = pl.DeviceIdType.MESH


def row_partner(shift, outer):
    return {"o": lax.rem(lax.axis_index("o") + shift, outer)}


def greet_partners(outer=1):
    barrier = pltpu.get_barrier_semaphore()
    partners = [{axis: 1 - lax.axis_index(axis)} for axis in group]
    partners += [row_partner(shift, outer) for shift in range(1, outer)]
    for partner in partners:
        pl.semaphore_signal(barrier, inc=1, device_id=partner, device_id_type=MESH)
    pl.semaphore_wait(barrier, len(partners))


def send_along(axis, source, target, semaphores, slot):
    return pltpu.make_async_remote_copy(
        src_ref=source,
        dst_ref=target,
        send_sem=semaphores.at[0, slot],
        recv_sem=semaphores.at[1, slot],
        device_id={axis: 1 - lax.axis_index(axis)},
        device_id_type=MESH,
    )


def first_row(flips, rows):
    i, y, c = [
        1 - lax.axis_index(axis) if axis in flips else lax.axis_index(axis) for axis in group
    ]
    return pl.multiple_of(((i * 2 + y) * 2 + c) * rows, rows)


def gather_kernel(outer, *refs):
    source, target, semaphores, own_semaphore = refs
    rows = source.shape[0]
    half = rows // 2
    greet_partners(outer)

    def place(flips, part=None):
        start = first_row(flips, rows)
        if part is None:
            return target.at[pl.ds(start, rows), :]
        return target.at[pl.ds(start + part * half, half), :]

    started = []

    def send(axis, source, target, slot):
        copy = send_along(axis, source, target, semaphores, slot)
        copy.start()
        started.append(copy)
        return copy

    own = pltpu.make_async_copy(source, place(()), own_semaphore)
    own.start()
    top, bottom = source.at[pl.ds(0, half), :], source.at[pl.ds(half, half), :]
    i_top = send("i", top, place((), 0), 0)
    y_bottom = send("y", bottom, place((), 1), 1)
    i_bottom = send("i", bottom, place((), 1), 2)
    y_top = send("y", top, place((), 0), 3)
    core = [send("c", source, place(()), 4)]
    i_top.wait_recv()
    across_top = send("y", place(("i",), 0), place(("i",), 0), 5)
    y_bottom.wait_recv()
    across_bottom = send("i", place(("y",), 1), place(("y",), 1), 6)
    i_bottom.wait_recv()
    core.append(send("c", place(("i",)), place(("i",)), 7))
    y_top.wait_recv()
    core.append(send("c", place(("y",)), place(("y",)), 8))
    across_top.wait_recv()
    core.append(send("c", place(("i", "y"), 0), place(("i", "y"), 0), 9))
    across_bottom.wait_recv()
    core.append(send("c", place(("i", "y"), 1), place(("i", "y"), 1), 10))
    for copy in core:
        copy.wait_recv()
    own.wait()
    for copy in started:
        copy.wait_send()


def opening_kernel(outer, token_ref, gain_ref, token_out, gain_out, *scratch):
    semaphores, own_semaphore, side_semaphores, row_semaphores = scratch
    me, side = lax.axis_index("o"), lax.axis_index("i")

    gather_kernel(outer, token_ref, token_out, semaphores, own_semaphore)
    gain_out[me * 2 + side] = gain_ref[...]
    along = send_along("i", gain_ref, gain_out.at[me * 2 + side], side_semaphores, 0)
    along.start()
    started = [along]

    def send_rows(source, slot, first):
        for shift in range(1, outer):
            copy = pltpu.make_async_remote_copy(
                src_ref=source,
                dst_ref=gain_out.at[slot],
                send_sem=row_semaphores.at[0, first, shift],
                recv_sem=row_semaphores.at[1, first, shift],
                device_id=row_partner(shift, outer),
                device_id_type=MESH,
            )
            copy.start()
            started.append(copy)

    send_rows(gain_ref, me * 2 + side, 0)
    along.wait_recv()
    send_rows(gain_out.at[me * 2 + 1 - side], me * 2 + 1 - side, 1)
    for copy in started[1:]:
        copy.wait_recv()
    for copy in started:
        copy.wait_send()


def opening_gather(array, gains, outer):
    rows, width = array.shape
    padded = jnp.pad(gains, ((0, 16 - gains.shape[0]), (0, 0)))
    vmem, hbm = pl.BlockSpec(memory_space=pltpu.VMEM), pl.BlockSpec(memory_space=pl.ANY)
    gathered, gain_rows = pl.pallas_call(
        lambda *refs: opening_kernel(outer, *refs),
        in_specs=[vmem] * 2,
        out_specs=[hbm, vmem],
        out_shape=[
            jax.ShapeDtypeStruct((8 * rows, width), array.dtype),
            jax.ShapeDtypeStruct((2 * outer, *padded.shape), gains.dtype),
        ],
        scratch_shapes=[
            pltpu.SemaphoreType.DMA((2, 11)),
            pltpu.SemaphoreType.DMA(()),
            pltpu.SemaphoreType.DMA((2, 1)),
            pltpu.SemaphoreType.DMA((2, 2, max(outer, 2))),
        ],
        compiler_params=pltpu.CompilerParams(collective_id=2, has_side_effects=True),
        cost_estimate=pl.CostEstimate(
            flops=0, bytes_accessed=200 * rows * width, transcendentals=0
        ),
        name="opening_gather",
    )(array, padded)
    return gathered, [gain_rows[:, which].reshape(-1) for which in range(2)]


def token_gather(array):
    rows, width = array.shape
    return pl.pallas_call(
        lambda *refs: gather_kernel(1, *refs),
        in_specs=[pl.BlockSpec(memory_space=pltpu.VMEM)],
        out_specs=pl.BlockSpec(memory_space=pl.ANY),
        out_shape=jax.ShapeDtypeStruct((8 * rows, width), array.dtype),
        scratch_shapes=[pltpu.SemaphoreType.DMA((2, 11)), pltpu.SemaphoreType.DMA(())],
        compiler_params=pltpu.CompilerParams(collective_id=1, has_side_effects=True),
        cost_estimate=pl.CostEstimate(
            flops=0, bytes_accessed=200 * rows * width, transcendentals=0
        ),
        name="token_gather",
    )(array)


class TokenSum:
    def __init__(self, windows, lefts, rights, total, scratch):
        self.windows, self.lefts, self.rights, self.total = windows, lefts, rights, total
        (
            self.left_held,
            self.right_held,
            self.core_out,
            self.core_in,
            self.sums,
            self.first_i,
            self.first_y,
            self.second_i,
            self.second_y,
            self.left_semaphores,
            self.right_semaphores,
            self.semaphores,
        ) = scratch
        rows, _ = total.shape
        half = rows // 2
        self.top, self.bottom = top, bottom = pl.ds(0, half), pl.ds(half, half)
        sums, first_i, first_y = self.sums, self.first_i, self.first_y
        plan = {
            "i1": ("i", sums.at[0, top, :], first_i.at[1], 4),
            "y1": ("y", sums.at[0, bottom, :], first_y.at[1], 5),
            "i0": ("i", sums.at[1, top, :], first_i.at[0], 6),
            "y0": ("y", sums.at[2, bottom, :], first_y.at[0], 7),
            "i2": ("i", sums.at[1, bottom, :], self.second_i, 8),
            "y2": ("y", sums.at[2, top, :], self.second_y, 9),
        }
        self.copies = {
            name: send_along(axis, source, target, self.semaphores, slot)
            for name, (axis, source, target, slot) in plan.items()
        }

    def core_copy(self, r):
        return send_along("c", self.core_out.at[r], self.core_in.at[r], self.semaphores, r)

    def right_copies(self):
        edge = 0
        for which, (_, start, depth) in enumerate(self.windows):
            yield pltpu.make_async_copy(
                self.rights[which].at[:, pl.ds(start, depth)],
                self.right_held.at[:, pl.ds(edge, depth)],
                self.right_semaphores.at[which],
            )
            edge += depth

    def left_copies(self, step, first):
        rows, edge = self.total.shape[0], 0
        for which, (start, _, depth) in enumerate(self.windows):
            yield pltpu.make_async_copy(
                self.lefts[which].at[pl.ds(first, rows), pl.ds(start, depth)],
                self.left_held.at[step, :, pl.ds(edge, depth)],
                self.left_semaphores.at[step, which],
            )
            edge += depth

    def load(self):
        for copy in self.right_copies():
            copy.start()
        rows = self.total.shape[0]
        for r, flips in enumerate((("i", "y"), ("i",), ("y",), ())):
            for mine, axes in enumerate((flips + ("c",), flips)):
                for copy in self.left_copies(2 * r + mine, first_row(axes, rows)):
                    copy.start()

    def add_to(self, r, part, arrived):
        self.sums[r, part, :] = (
            self.sums[r, part, :].astype(jnp.float32) + arrived.astype(jnp.float32)
        ).astype(jnp.bfloat16)

    def second(self):
        self.copies["y1"].wait_recv()
        self.add_to(1, self.bottom, self.first_y[1])
        self.copies["i2"].start()
        self.copies["i1"].wait_recv()
        self.add_to(2, self.top, self.first_i[1])
        self.copies["y2"].start()

    def run(self, second_inside):
        width = self.total.shape[1]
        tile = 512
        for copy in self.right_copies():
            copy.wait()

        def product(step, t):
            columns = pl.ds(pl.multiple_of(t * tile, tile), tile)
            return columns, contract(
                self.left_held[step], self.right_held[columns, :], 1, 1
            )

        def one_relation(r, carry):
            for copy in self.left_copies(2 * r, 0):
                copy.wait()

            def sibling_tile(t, inner):
                columns, value = product(2 * r, t)
                self.core_out[r, :, columns] = value.astype(jnp.bfloat16)
                return inner

            lax.fori_loop(0, width // tile, sibling_tile, 0)
            self.core_copy(r).start()
            for copy in self.left_copies(2 * r + 1, 0):
                copy.wait()
            self.core_copy(r).wait_recv()

            def own_tile(t, inner):
                columns, value = product(2 * r + 1, t)
                value = value + self.core_in[r, :, columns].astype(jnp.float32)

                @pl.when(r < 3)
                def _():
                    self.sums[r, :, columns] = value.astype(jnp.bfloat16)

                @pl.when(r == 3)
                def _():
                    self.total[:, columns] = value

                return inner

            lax.fori_loop(0, width // tile, own_tile, 0)

            @pl.when(r == 0)
            def _():
                self.copies["i1"].start()
                self.copies["y1"].start()

            @pl.when(r == 1)
            def _():
                self.copies["i0"].start()

            @pl.when(r == 2)
            def _():
                self.copies["y0"].start()
                if second_inside:
                    self.second()

            return carry

        lax.fori_loop(0, 4, one_relation, 0)

    def finish(self):
        self.copies["i0"].wait_recv()
        self.total[self.top, :] += self.first_i[0].astype(jnp.float32)
        self.copies["y0"].wait_recv()
        self.total[self.bottom, :] += self.first_y[0].astype(jnp.float32)
        self.copies["y2"].wait_recv()
        self.total[self.top, :] += self.second_y[...].astype(jnp.float32)
        self.copies["i2"].wait_recv()
        self.total[self.bottom, :] += self.second_i[...].astype(jnp.float32)

    def drain(self):
        for copy in self.copies.values():
            copy.wait_send()
        for r in range(4):
            self.core_copy(r).wait_send()


def sum_scratch(terms):
    rows, width = terms[0][0].shape[0] // 8, terms[0][2].shape[0]
    half, depth, count = rows // 2, sum(term[4] for term in terms), len(terms)
    return [
        pltpu.VMEM((8, rows, depth), jnp.bfloat16),
        pltpu.VMEM((width, depth), jnp.bfloat16),
        pltpu.VMEM((4, rows, width), jnp.bfloat16),
        pltpu.VMEM((4, rows, width), jnp.bfloat16),
        pltpu.VMEM((4, rows, width), jnp.bfloat16),
        pltpu.VMEM((2, half, width), jnp.bfloat16),
        pltpu.VMEM((2, half, width), jnp.bfloat16),
        pltpu.VMEM((half, width), jnp.bfloat16),
        pltpu.VMEM((half, width), jnp.bfloat16),
        pltpu.SemaphoreType.DMA((8, count)),
        pltpu.SemaphoreType.DMA((count,)),
        pltpu.SemaphoreType.DMA((2, 10)),
    ]


def sum_operands(terms):
    return [term[0] for term in terms] + [term[2] for term in terms]


def sum_steps(terms, operands, total, scratch):
    windows = [(term[1], term[3], term[4]) for term in terms]
    return TokenSum(windows, operands[: len(terms)], operands[len(terms) :], total, scratch)


def sum_flops(terms):
    return sum(2 * t[0].shape[0] * t[2].shape[0] * t[4] for t in terms)


def product_sum(terms, number):
    rows, width = terms[0][0].shape[0] // 8, terms[0][2].shape[0]
    count = 2 * len(terms)

    def kernel(*refs):
        steps = sum_steps(terms, refs[:count], refs[count], refs[count + 1 :])
        steps.load()
        greet_partners()
        steps.run(True)
        steps.finish()
        steps.drain()

    return pl.pallas_call(
        kernel,
        in_specs=[pl.BlockSpec(memory_space=pl.ANY)] * count,
        out_specs=pl.BlockSpec(memory_space=pltpu.VMEM),
        out_shape=jax.ShapeDtypeStruct((rows, width), jnp.float32),
        scratch_shapes=sum_scratch(terms),
        compiler_params=pltpu.CompilerParams(collective_id=number, has_side_effects=True),
        cost_estimate=pl.CostEstimate(
            flops=sum_flops(terms), bytes_accessed=100 * rows * width, transcendentals=0
        ),
    )(*sum_operands(terms))


def input_gradient(terms, inputs, grad_hidden, gain):
    rows, width = inputs.shape
    count = 2 * len(terms)
    tile = 32

    def kernel(*refs):
        input_ref, grad_hidden_ref, gain_ref, grad_out, part_out = refs[count : count + 5]
        steps = sum_steps(terms, refs[:count], grad_out, refs[count + 5 :])
        steps.load()
        greet_partners()
        steps.run(True)
        steps.finish()

        def one_tile(t, part):
            span = pl.ds(pl.multiple_of(t * tile, tile), tile)
            values = input_ref[span, :].astype(jnp.float32)
            inverse = inverse_rms(values)
            normed = values * inverse
            grad_normed = grad_out[span, :]
            scaled = grad_normed * gain_ref[...]
            mean = jnp.mean(scaled * normed, axis=-1, keepdims=True)
            grad_out[span, :] = grad_hidden_ref[span, :] + inverse * (scaled - normed * mean)
            return part + jnp.sum(grad_normed * normed, axis=0, keepdims=True)

        part_out[...] = lax.fori_loop(
            0, rows // tile, one_tile, jnp.zeros((1, width), jnp.float32)
        )
        steps.drain()

    vmem, hbm = pl.BlockSpec(memory_space=pltpu.VMEM), pl.BlockSpec(memory_space=pl.ANY)
    return pl.pallas_call(
        kernel,
        in_specs=[hbm] * count + [vmem] * 3,
        out_specs=[vmem] * 2,
        out_shape=[
            jax.ShapeDtypeStruct((rows, width), jnp.float32),
            jax.ShapeDtypeStruct((1, width), jnp.float32),
        ],
        scratch_shapes=sum_scratch(terms),
        compiler_params=pltpu.CompilerParams(collective_id=6, has_side_effects=True),
        cost_estimate=pl.CostEstimate(
            flops=sum_flops(terms), bytes_accessed=150 * rows * width, transcendentals=rows
        ),
        name="input_gradient",
    )(*sum_operands(terms), inputs, grad_hidden, gain.reshape(1, width))


def closing(terms, hidden, parts, outer):
    rows, width = hidden.shape
    count = 2 * len(terms)

    def kernel(*refs):
        hidden_ref, part_ref, layer_out, total_out = refs[count : count + 4]
        scratch = refs[count + 4 :]
        held, stages, semaphores, row_semaphores = scratch[-4:]
        output = sum_steps(terms, refs[:count], layer_out, scratch[:-4])
        output.load()
        greet_partners(outer)
        started = []

        def pass_on(step, source):
            copy = send_along(group[step], source, held.at[step], semaphores, step)
            copy.start()
            started.append(copy)

        pass_on(0, part_ref)
        output.run(False)
        value = part_ref[...]
        for step in range(3):
            started[step].wait_recv()
            value = value + held[step]
            stages[step] = value
            if step < 2:
                pass_on(step + 1, stages.at[step])
        for shift in range(1, outer):
            copy = pltpu.make_async_remote_copy(
                src_ref=stages.at[2],
                dst_ref=held.at[2 + shift],
                send_sem=row_semaphores.at[0, shift],
                recv_sem=row_semaphores.at[1, shift],
                device_id=row_partner(shift, outer),
                device_id_type=MESH,
            )
            copy.start()
            started.append(copy)
        output.second()
        output.finish()
        layer_out[...] += hidden_ref[...]
        value = stages[2]
        for shift in range(1, outer):
            started[2 + shift].wait_recv()
            value = value + held[2 + shift]
        total_out[...] = value
        for copy in started:
            copy.wait_send()
        output.drain()

    vmem, hbm = pl.BlockSpec(memory_space=pltpu.VMEM), pl.BlockSpec(memory_space=pl.ANY)
    return pl.pallas_call(
        kernel,
        in_specs=[hbm] * count + [vmem] * 2,
        out_specs=[vmem] * 2,
        out_shape=[
            jax.ShapeDtypeStruct((rows, width), jnp.float32),
            jax.ShapeDtypeStruct(parts.shape, jnp.float32),
        ],
        scratch_shapes=[
            *sum_scratch(terms),
            pltpu.VMEM((2 + outer, *parts.shape), jnp.float32),
            pltpu.VMEM((3, *parts.shape), jnp.float32),
            pltpu.SemaphoreType.DMA((2, 3)),
            pltpu.SemaphoreType.DMA((2, max(outer, 2))),
        ],
        compiler_params=pltpu.CompilerParams(collective_id=5, has_side_effects=True),
        cost_estimate=pl.CostEstimate(
            flops=sum_flops(terms), bytes_accessed=150 * rows * width, transcendentals=0
        ),
        name="closing",
    )(*sum_operands(terms), hidden, parts)


def rope_tables():
    half_dim = HD // 2
    lanes = jnp.arange(PAIR)
    inverse = rope_base ** (-((lanes % half_dim).astype(jnp.float32) * 2.0 / HD))
    angles = jnp.arange(LEN, dtype=jnp.float32)[:, None] * inverse[None, :]
    sign = jnp.where(lanes % HD < half_dim, -1.0, 1.0)
    return jnp.cos(angles), jnp.sin(angles) * sign[None, :]


def turn(values, cosine, signed_sine):
    half_dim = HD // 2
    lanes = lax.broadcasted_iota(jnp.int32, values.shape, 1)
    other = jnp.where(
        lanes % HD < half_dim,
        pltpu.roll(values, PAIR - half_dim, 1),
        pltpu.roll(values, half_dim, 1),
    )
    return values * cosine + other * signed_sine


def head_parts(values):
    lanes = lax.broadcasted_iota(jnp.int32, values.shape, 1)
    empty = jnp.zeros_like(values)
    return [jnp.where(lanes // HD == head, values, empty) for head in range(2)]


def forward_kernel(
    query_ref, key_ref, value_ref, cos_ref, sin_ref, q_out, k_out, v_out, attended_out
):
    cosine, sine = cos_ref[...], sin_ref[...]
    queries = turn(query_ref[...], cosine, sine).astype(jnp.bfloat16)
    keys = turn(key_ref[...], cosine, sine).astype(jnp.bfloat16)
    values = value_ref[...].astype(jnp.bfloat16)
    q_out[...] = queries
    k_out[...] = keys
    v_out[...] = values
    value_parts = head_parts(values)
    scaling = HD**-0.5
    for block in range(LEN // BLK):
        rows = slice(block * BLK, (block + 1) * BLK)
        seen = (block + 1) * BLK
        total = None
        for head, query_part in enumerate(head_parts(queries[rows])):
            scores = contract(query_part, keys[:seen], 1, 1) * scaling
            top = jnp.max(scores, axis=-1, keepdims=True)
            powers = jnp.exp(scores - top)
            weights = powers / jnp.sum(powers, axis=-1, keepdims=True)
            term = contract(weights.astype(jnp.bfloat16), value_parts[head][:seen], 1, 0)
            total = term if total is None else total + term
        attended_out[rows, :] = total.astype(jnp.bfloat16)


def backward_kernel(
    query_ref, key_ref, value_ref, grad_ref, cos_ref, sin_ref, q_out, k_out, v_out, key_acc, value_acc
):
    keys, values = key_ref[...], value_ref[...]
    key_parts = head_parts(keys)
    scaling = HD**-0.5
    key_acc[...] = jnp.zeros_like(key_acc)
    value_acc[...] = jnp.zeros_like(value_acc)
    for block in range(LEN // BLK):
        rows = slice(block * BLK, (block + 1) * BLK)
        seen = (block + 1) * BLK
        query_parts = head_parts(query_ref[rows, :])
        grad_parts = head_parts(grad_ref[rows, :])
        query_delta = None
        for head in range(2):
            scores = contract(query_parts[head], keys[:seen], 1, 1) * scaling
            top = jnp.max(scores, axis=-1, keepdims=True)
            powers = jnp.exp(scores - top)
            weights = powers / jnp.sum(powers, axis=-1, keepdims=True)
            grad_probs = contract(grad_parts[head], values[:seen], 1, 1)
            row_dot = jnp.sum(weights * grad_probs, axis=-1, keepdims=True)
            grad_scores = (weights * (grad_probs - row_dot) * scaling).astype(jnp.bfloat16)
            term = contract(grad_scores, key_parts[head][:seen], 1, 0)
            query_delta = term if query_delta is None else query_delta + term
            key_acc[:seen, :] += contract(grad_scores, query_parts[head], 0, 0)
            value_acc[:seen, :] += contract(weights.astype(jnp.bfloat16), grad_parts[head], 0, 0)
        q_out[rows, :] = turn(query_delta, cos_ref[rows, :], -sin_ref[rows, :]).astype(jnp.bfloat16)
    k_out[...] = turn(key_acc[...], cos_ref[...], -sin_ref[...]).astype(jnp.bfloat16)
    v_out[...] = value_acc[...].astype(jnp.bfloat16)


def attention_cost(rows, width, products):
    return pl.CostEstimate(
        flops=2 * products * rows * LEN * width,
        bytes_accessed=8 * rows * width * 2,
        transcendentals=rows * LEN * width // HD,
    )


def attention_forward(mixed, tables):
    rows, width = mixed.shape[0], mixed.shape[1] // 3
    pairs = width // PAIR

    def part(which):
        return pl.BlockSpec((LEN, PAIR), lambda s, p: (s, which * pairs + p))

    whole = pl.BlockSpec((LEN, PAIR), lambda s, p: (0, 0))
    return pl.pallas_call(
        forward_kernel,
        grid=(rows // LEN, pairs),
        in_specs=[part(0), part(1), part(2), whole, whole],
        out_specs=[part(0)] * 4,
        out_shape=[jax.ShapeDtypeStruct((rows, width), jnp.bfloat16)] * 4,
        cost_estimate=attention_cost(rows, width, 2),
        name="attention_forward",
    )(mixed, mixed, mixed, *tables)


def attention_backward(queries, keys, values, grads, tables):
    rows, width = queries.shape
    part = pl.BlockSpec((LEN, PAIR), lambda s, p: (s, p))
    whole = pl.BlockSpec((LEN, PAIR), lambda s, p: (0, 0))
    return pl.pallas_call(
        backward_kernel,
        grid=(rows // LEN, width // PAIR),
        in_specs=[part] * 4 + [whole] * 2,
        out_specs=[part] * 3,
        out_shape=[jax.ShapeDtypeStruct((rows, width), jnp.bfloat16)] * 3,
        scratch_shapes=[pltpu.VMEM((LEN, PAIR), jnp.float32)] * 2,
        cost_estimate=attention_cost(rows, width, 5),
        name="attention_backward",
    )(queries, keys, values, grads, *tables)


def feed_kernel(normed_ref, cotangent_ref, weight_ref, out_ref):
    chunk = out_ref.shape[1] // 3
    gate, up, down = [slice(which * chunk, (which + 1) * chunk) for which in range(3)]
    gate_pre = contract(normed_ref[...], weight_ref[:, gate], 1, 0)
    up_proj = contract(normed_ref[...], weight_ref[:, up], 1, 0)
    grad_act = contract(cotangent_ref[...], weight_ref[:, down], 1, 0)
    sigmoid_gate = jax.nn.sigmoid(gate_pre)
    silu_gate = gate_pre * sigmoid_gate
    gate_slope = sigmoid_gate * (1.0 + gate_pre * (1.0 - sigmoid_gate))
    out_ref[:, gate] = (grad_act * up_proj * gate_slope).astype(jnp.bfloat16)
    out_ref[:, up] = (grad_act * silu_gate).astype(jnp.bfloat16)
    out_ref[:, down] = (silu_gate * up_proj).astype(jnp.bfloat16)


def feed_units(normed, cotangents, weights):
    (rows, width), columns = normed.shape, weights.shape[1]
    tile = 256
    tokens = pl.BlockSpec((tile, width), lambda t: (t, 0))
    return pl.pallas_call(
        feed_kernel,
        grid=(rows // tile,),
        in_specs=[tokens, tokens, pl.BlockSpec((width, columns), lambda t: (0, 0))],
        out_specs=pl.BlockSpec((tile, columns), lambda t: (t, 0)),
        out_shape=jax.ShapeDtypeStruct((rows, columns), jnp.bfloat16),
        cost_estimate=pl.CostEstimate(
            flops=2 * rows * width * columns,
            bytes_accessed=2 * (2 * rows * width + width * columns + rows * columns),
            transcendentals=rows * columns // 3,
        ),
        name="feed_units",
    )(normed, cotangents, weights)


def weight_grads(terms):
    rows, width = terms[0][0].shape
    tile = 256
    operands, specs, plan = [], [], []
    for left, rights in terms:
        operands.append(left)
        specs.append(pl.BlockSpec((rows, tile), lambda t: (0, t)))
        for right, start, columns in rights:
            operands.append(right)
            specs.append(
                pl.BlockSpec((rows, columns), lambda t, block=start // columns: (0, block))
            )
        plan.append([columns for _, _, columns in rights])
    total = sum(sum(widths) for widths in plan)

    def kernel(*refs):
        edge, at = 0, 0
        for widths in plan:
            left = refs[at][...]
            at += 1
            for columns in widths:
                refs[-1][:, edge : edge + columns] = contract(left, refs[at][...], 0, 0).astype(
                    jnp.bfloat16
                )
                edge += columns
                at += 1

    return pl.pallas_call(
        kernel,
        grid=(width // tile,),
        in_specs=specs,
        out_specs=pl.BlockSpec((tile, total), lambda t: (t, 0)),
        out_shape=jax.ShapeDtypeStruct((width, total), jnp.bfloat16),
        cost_estimate=pl.CostEstimate(
            flops=2 * rows * width * total,
            bytes_accessed=2 * (2 * rows * width + width * total + rows * total),
            transcendentals=0,
        ),
    )(*operands)


def exchange_rows(weights, first, width):
    side = lax.axis_index("i")

    def columns(half):
        start = [half * (w.shape[1] // 2) + first for w in weights]
        return jnp.concatenate([w[:, a : a + width] for w, a in zip(weights, start)], axis=1)

    low, high = columns(0), columns(1)
    kept = jnp.where(side == 0, low, high)
    other = lax.ppermute(jnp.where(side == 0, high, low), "i", swap)
    return jnp.concatenate(
        [jnp.where(side == 0, kept, other), jnp.where(side == 0, other, kept)]
    )


def row_gather(values):
    return lax.all_gather(values, "o", axis=0, tiled=True)


def row_sum(partial_value):
    return lax.psum_scatter(partial_value, "o", scatter_dimension=0, tiled=True)


def exchange_columns(summed):
    side = lax.axis_index("i")
    rows = summed.shape[0] // 2
    kept = lax.dynamic_slice_in_dim(summed, side * rows, rows, axis=0)
    other = lax.ppermute(
        lax.dynamic_slice_in_dim(summed, (1 - side) * rows, rows, axis=0), "i", swap
    )
    return kept, other


def in_order(halves):
    kept, other = halves
    side = lax.axis_index("i")
    return jnp.where(side == 0, kept, other), jnp.where(side == 0, other, kept)


def inverse_rms(values):
    return lax.rsqrt(jnp.mean(values * values, axis=-1, keepdims=True) + epsilon)


def per_device(
    layer_input,
    query_weight,
    key_weight,
    value_weight,
    out_weight,
    gate_weight,
    up_weight,
    down_weight,
    attention_gain,
    feed_gain,
    out_cotangent,
):
    head_width = query_weight.shape[1] // 2
    hidden = gate_weight.shape[1] // 2
    chunk = hidden // CHUNKS
    tables = rope_tables()
    outer = lax.axis_size("o")

    attention_rows = exchange_rows(
        (query_weight, key_weight, value_weight, out_weight), 0, head_width
    )
    attention_full = row_gather(attention_rows)
    feed_full = []
    for k in range(CHUNKS):
        feed_rows = exchange_rows((gate_weight, up_weight, down_weight), k * chunk, chunk)
        feed_full.append(row_gather(feed_rows))
    inputs_all, gains = opening_gather(layer_input, jnp.stack([attention_gain, feed_gain]), outer)
    gain_one, gain_two = [g.astype(jnp.float32) for g in gains]
    inputs_all = inputs_all.astype(jnp.float32)
    normed = (inputs_all * inverse_rms(inputs_all) * gain_one).astype(jnp.bfloat16)
    normed, tables, late = lax.optimization_barrier((normed, tables, out_cotangent))
    cotangents = token_gather(late)
    inputs = layer_input.astype(jnp.float32)

    mixed = contract(normed, attention_full[:, : 3 * head_width], 1, 0)
    queries, keys, values, attended = attention_forward(mixed, tables)
    out_full = attention_full[:, 3 * head_width :]
    hidden_state = inputs + product_sum(
        [(attended, 0, attention_full, 3 * head_width, head_width)], 3
    )
    inv_two = inverse_rms(hidden_state)
    normed_two_raw = hidden_state * inv_two
    normed_two = token_gather((normed_two_raw * gain_two).astype(jnp.bfloat16))

    output_terms, grad_terms, feed_grads = [], [], []
    for k in range(CHUNKS):
        units = feed_units(normed_two, cotangents, feed_full[k])
        grads = weight_grads(
            [
                (normed_two, [(units, 0, 2 * chunk)]),
                (cotangents, [(units, 2 * chunk, chunk)]),
            ],
        )
        units, grads, normed_two, cotangents = lax.optimization_barrier(
            (units, grads, normed_two, cotangents)
        )
        summed = row_sum(grads)
        feed_grads.append(exchange_columns(summed))
        grad_terms.append((units, 0, feed_full[k], 0, 2 * chunk))
        output_terms.append((units, 2 * chunk, feed_full[k], 2 * chunk, chunk))

    grad_normed_two = product_sum(grad_terms, 4)
    feed_gain_part = jnp.sum(grad_normed_two * normed_two_raw, axis=0, keepdims=True)
    scaled_two = grad_normed_two * gain_two
    grad_hidden = out_cotangent.astype(jnp.float32) + inv_two * (
        scaled_two - normed_two_raw * jnp.mean(scaled_two * normed_two_raw, axis=-1, keepdims=True)
    )
    grad_rows = token_gather(grad_hidden.astype(jnp.bfloat16))
    grad_attended = contract(grad_rows, out_full, 1, 0).astype(jnp.bfloat16)
    grad_query, grad_key, grad_value = attention_backward(
        queries, keys, values, grad_attended, tables
    )
    attention_grads = weight_grads(
        [
            (normed, [(g, 0, head_width) for g in (grad_query, grad_key, grad_value)]),
            (grad_rows, [(attended, 0, head_width)]),
        ],
    )
    attention_grads, grad_query = lax.optimization_barrier((attention_grads, grad_query))
    attention_summed = row_sum(attention_grads)
    attention_halves = exchange_columns(attention_summed)
    input_grad, attention_gain_part = input_gradient(
        [
            (g, 0, attention_full, which * head_width, head_width)
            for which, g in enumerate((grad_query, grad_key, grad_value))
        ],
        layer_input,
        grad_hidden,
        gain_one,
    )
    parts = jnp.concatenate([attention_gain_part, feed_gain_part, jnp.zeros((6, feed_gain_part.shape[1]))])
    layer_output, gain_sums = closing(output_terms, hidden_state, parts, outer)

    def whole_rows(halves, which, width):
        return jnp.concatenate(
            [
                half[k][:, which * width : (which + 1) * width]
                for half in zip(*halves)
                for k in range(len(halves))
            ],
            axis=1,
        ).astype(jnp.float32)

    feed_halves = [in_order(halves) for halves in feed_grads]
    feed_rows = [whole_rows(feed_halves, which, chunk) for which in range(3)]
    attention_halves = [in_order(attention_halves)]
    attention_rows = [whole_rows(attention_halves, which, head_width) for which in range(4)]
    device = lax.axis_index("o")
    for axis in group:
        device = device * 2 + lax.axis_index(axis)
    share = attention_gain.shape[0] // 4
    gain_grads = [
        lax.dynamic_slice_in_dim(gain_sums[which], device * share, share) for which in range(2)
    ]
    return (
        layer_output,
        input_grad,
        *attention_rows,
        *feed_rows,
        *gain_grads,
    )


def solution(mesh):
    rows, columns = mesh.shape["dp"], mesh.shape["tensor"]
    fine = Mesh(
        mesh.devices.reshape(rows // 2, 2, columns // 2, 2), ("o", "i", "y", "c")
    )
    tokens = P(("o", "i", "y", "c"), None)
    weight = P(("o", "i"), ("y", "c"))
    gain = P(("o", "i"))

    return jax.shard_map(
        per_device,
        mesh=fine,
        in_specs=(tokens, *[weight] * 7, gain, gain, tokens),
        out_specs=(tokens, tokens, *[weight] * 7, P(("o", "i", "y", "c")), P(("o", "i", "y", "c"))),
        check_vma=False,
    )
```

```python
import jax
import jax.numpy as jnp
from jax import lax
from jax.experimental import pallas as pl
from jax.experimental.pallas import tpu as pltpu
from jax.sharding import Mesh, PartitionSpec as P

HD = 64
LEN = 1024
BLK = 256
PAIR = 2 * HD
EIGHTHS = (6, 2)

epsilon = 1e-05
rope_base = 130000.0
group = ("i", "y", "c")
swap = [(0, 1), (1, 0)]


def contract(left_side, right_side, left_dim, right_dim):
    return lax.dot_general(
        left_side,
        right_side,
        (((left_dim,), (right_dim,)), ((), ())),
        preferred_element_type=jnp.float32,
    )


MESH = pl.DeviceIdType.MESH


def row_partner(shift, outer):
    return {"o": lax.rem(lax.axis_index("o") + shift, outer)}


def greet_partners(outer=1):
    barrier = pltpu.get_barrier_semaphore()
    partners = [{axis: 1 - lax.axis_index(axis)} for axis in group]
    partners += [row_partner(shift, outer) for shift in range(1, outer)]
    for partner in partners:
        pl.semaphore_signal(barrier, inc=1, device_id=partner, device_id_type=MESH)
    pl.semaphore_wait(barrier, len(partners))


def send_along(axis, source, target, semaphores, slot):
    return pltpu.make_async_remote_copy(
        src_ref=source,
        dst_ref=target,
        send_sem=semaphores.at[0, slot],
        recv_sem=semaphores.at[1, slot],
        device_id={axis: 1 - lax.axis_index(axis)},
        device_id_type=MESH,
    )


def first_row(flips, rows):
    i, y, c = [
        1 - lax.axis_index(axis) if axis in flips else lax.axis_index(axis) for axis in group
    ]
    return pl.multiple_of(((i * 2 + y) * 2 + c) * rows, rows)


def gather_kernel(outer, *refs):
    source, target, semaphores, own_semaphore = refs
    rows = source.shape[0]
    half = rows // 2
    greet_partners(outer)

    def place(flips, part=None):
        start = first_row(flips, rows)
        if part is None:
            return target.at[pl.ds(start, rows), :]
        return target.at[pl.ds(start + part * half, half), :]

    started = []

    def send(axis, source, target, slot):
        copy = send_along(axis, source, target, semaphores, slot)
        copy.start()
        started.append(copy)
        return copy

    own = pltpu.make_async_copy(source, place(()), own_semaphore)
    own.start()
    top, bottom = source.at[pl.ds(0, half), :], source.at[pl.ds(half, half), :]
    i_top = send("i", top, place((), 0), 0)
    y_bottom = send("y", bottom, place((), 1), 1)
    i_bottom = send("i", bottom, place((), 1), 2)
    y_top = send("y", top, place((), 0), 3)
    core = [send("c", source, place(()), 4)]
    i_top.wait_recv()
    across_top = send("y", place(("i",), 0), place(("i",), 0), 5)
    y_bottom.wait_recv()
    across_bottom = send("i", place(("y",), 1), place(("y",), 1), 6)
    i_bottom.wait_recv()
    core.append(send("c", place(("i",)), place(("i",)), 7))
    y_top.wait_recv()
    core.append(send("c", place(("y",)), place(("y",)), 8))
    across_top.wait_recv()
    core.append(send("c", place(("i", "y"), 0), place(("i", "y"), 0), 9))
    across_bottom.wait_recv()
    core.append(send("c", place(("i", "y"), 1), place(("i", "y"), 1), 10))
    for copy in core:
        copy.wait_recv()
    own.wait()
    for copy in started:
        copy.wait_send()


def opening_kernel(outer, token_ref, gain_ref, token_out, gain_out, *scratch):
    semaphores, own_semaphore, side_semaphores, row_semaphores = scratch
    me, side = lax.axis_index("o"), lax.axis_index("i")

    gather_kernel(outer, token_ref, token_out, semaphores, own_semaphore)
    gain_out[me * 2 + side] = gain_ref[...]
    along = send_along("i", gain_ref, gain_out.at[me * 2 + side], side_semaphores, 0)
    along.start()
    started = [along]

    def send_rows(source, slot, first):
        for shift in range(1, outer):
            copy = pltpu.make_async_remote_copy(
                src_ref=source,
                dst_ref=gain_out.at[slot],
                send_sem=row_semaphores.at[0, first, shift],
                recv_sem=row_semaphores.at[1, first, shift],
                device_id=row_partner(shift, outer),
                device_id_type=MESH,
            )
            copy.start()
            started.append(copy)

    send_rows(gain_ref, me * 2 + side, 0)
    along.wait_recv()
    send_rows(gain_out.at[me * 2 + 1 - side], me * 2 + 1 - side, 1)
    for copy in started[1:]:
        copy.wait_recv()
    for copy in started:
        copy.wait_send()


def opening_gather(array, gains, outer):
    rows, width = array.shape
    padded = jnp.pad(gains, ((0, 16 - gains.shape[0]), (0, 0)))
    vmem, hbm = pl.BlockSpec(memory_space=pltpu.VMEM), pl.BlockSpec(memory_space=pl.ANY)
    gathered, gain_rows = pl.pallas_call(
        lambda *refs: opening_kernel(outer, *refs),
        in_specs=[vmem] * 2,
        out_specs=[hbm, vmem],
        out_shape=[
            jax.ShapeDtypeStruct((8 * rows, width), array.dtype),
            jax.ShapeDtypeStruct((2 * outer, *padded.shape), gains.dtype),
        ],
        scratch_shapes=[
            pltpu.SemaphoreType.DMA((2, 11)),
            pltpu.SemaphoreType.DMA(()),
            pltpu.SemaphoreType.DMA((2, 1)),
            pltpu.SemaphoreType.DMA((2, 2, max(outer, 2))),
        ],
        compiler_params=pltpu.CompilerParams(collective_id=2, has_side_effects=True),
        cost_estimate=pl.CostEstimate(
            flops=0, bytes_accessed=200 * rows * width, transcendentals=0
        ),
        name="opening_gather",
    )(array, padded)
    return gathered, [gain_rows[:, which].reshape(-1) for which in range(2)]


def token_gather(array):
    rows, width = array.shape
    return pl.pallas_call(
        lambda *refs: gather_kernel(1, *refs),
        in_specs=[pl.BlockSpec(memory_space=pltpu.VMEM)],
        out_specs=pl.BlockSpec(memory_space=pl.ANY),
        out_shape=jax.ShapeDtypeStruct((8 * rows, width), array.dtype),
        scratch_shapes=[pltpu.SemaphoreType.DMA((2, 11)), pltpu.SemaphoreType.DMA(())],
        compiler_params=pltpu.CompilerParams(collective_id=1, has_side_effects=True),
        cost_estimate=pl.CostEstimate(
            flops=0, bytes_accessed=200 * rows * width, transcendentals=0
        ),
        name="token_gather",
    )(array)


class TokenSum:
    def __init__(self, windows, lefts, rights, total, scratch):
        self.windows, self.lefts, self.rights, self.total = windows, lefts, rights, total
        (
            self.left_held,
            self.right_held,
            self.core_out,
            self.core_in,
            self.sums,
            self.first_i,
            self.first_y,
            self.second_i,
            self.second_y,
            self.left_semaphores,
            self.right_semaphores,
            self.semaphores,
        ) = scratch
        rows, _ = total.shape
        half = rows // 2
        self.top, self.bottom = top, bottom = pl.ds(0, half), pl.ds(half, half)
        sums, first_i, first_y = self.sums, self.first_i, self.first_y
        plan = {
            "i1": ("i", sums.at[0, top, :], first_i.at[1], 4),
            "y1": ("y", sums.at[0, bottom, :], first_y.at[1], 5),
            "i0": ("i", sums.at[1, top, :], first_i.at[0], 6),
            "y0": ("y", sums.at[2, bottom, :], first_y.at[0], 7),
            "i2": ("i", sums.at[1, bottom, :], self.second_i, 8),
            "y2": ("y", sums.at[2, top, :], self.second_y, 9),
        }
        self.copies = {
            name: send_along(axis, source, target, self.semaphores, slot)
            for name, (axis, source, target, slot) in plan.items()
        }

    def core_copy(self, r):
        return send_along("c", self.core_out.at[r], self.core_in.at[r], self.semaphores, r)

    def right_copies(self):
        edge = 0
        for which, (_, start, depth) in enumerate(self.windows):
            yield pltpu.make_async_copy(
                self.rights[which].at[:, pl.ds(start, depth)],
                self.right_held.at[:, pl.ds(edge, depth)],
                self.right_semaphores.at[which],
            )
            edge += depth

    def left_copies(self, step, first):
        rows, edge = self.total.shape[0], 0
        for which, (start, _, depth) in enumerate(self.windows):
            yield pltpu.make_async_copy(
                self.lefts[which].at[pl.ds(first, rows), pl.ds(start, depth)],
                self.left_held.at[step, :, pl.ds(edge, depth)],
                self.left_semaphores.at[step, which],
            )
            edge += depth

    def load(self):
        for copy in self.right_copies():
            copy.start()
        rows = self.total.shape[0]
        for r, flips in enumerate((("i", "y"), ("i",), ("y",), ())):
            for mine, axes in enumerate((flips + ("c",), flips)):
                for copy in self.left_copies(2 * r + mine, first_row(axes, rows)):
                    copy.start()

    def add_to(self, r, part, arrived):
        self.sums[r, part, :] = (
            self.sums[r, part, :].astype(jnp.float32) + arrived.astype(jnp.float32)
        ).astype(jnp.bfloat16)

    def second(self):
        self.copies["y1"].wait_recv()
        self.add_to(1, self.bottom, self.first_y[1])
        self.copies["i2"].start()
        self.copies["i1"].wait_recv()
        self.add_to(2, self.top, self.first_i[1])
        self.copies["y2"].start()

    def run(self, second_inside):
        width = self.total.shape[1]
        tile = 1024
        for copy in self.right_copies():
            copy.wait()

        def product(step, t):
            columns = pl.ds(pl.multiple_of(t * tile, tile), tile)
            return columns, contract(
                self.left_held[step], self.right_held[columns, :], 1, 1
            )

        def one_relation(r, carry):
            for copy in self.left_copies(2 * r, 0):
                copy.wait()

            def sibling_tile(t, inner):
                columns, value = product(2 * r, t)
                self.core_out[r, :, columns] = value.astype(jnp.bfloat16)
                return inner

            lax.fori_loop(0, width // tile, sibling_tile, 0)
            self.core_copy(r).start()
            for copy in self.left_copies(2 * r + 1, 0):
                copy.wait()
            self.core_copy(r).wait_recv()

            def own_tile(t, inner):
                columns, value = product(2 * r + 1, t)
                value = value + self.core_in[r, :, columns].astype(jnp.float32)

                @pl.when(r < 3)
                def _():
                    self.sums[r, :, columns] = value.astype(jnp.bfloat16)

                @pl.when(r == 3)
                def _():
                    self.total[:, columns] = value

                return inner

            lax.fori_loop(0, width // tile, own_tile, 0)

            @pl.when(r == 0)
            def _():
                self.copies["i1"].start()
                self.copies["y1"].start()

            @pl.when(r == 1)
            def _():
                self.copies["i0"].start()

            @pl.when(r == 2)
            def _():
                self.copies["y0"].start()
                if second_inside:
                    self.second()

            return carry

        lax.fori_loop(0, 4, one_relation, 0)

    def finish(self):
        self.copies["i0"].wait_recv()
        self.total[self.top, :] += self.first_i[0].astype(jnp.float32)
        self.copies["y0"].wait_recv()
        self.total[self.bottom, :] += self.first_y[0].astype(jnp.float32)
        self.copies["y2"].wait_recv()
        self.total[self.top, :] += self.second_y[...].astype(jnp.float32)
        self.copies["i2"].wait_recv()
        self.total[self.bottom, :] += self.second_i[...].astype(jnp.float32)

    def drain(self):
        for copy in self.copies.values():
            copy.wait_send()
        for r in range(4):
            self.core_copy(r).wait_send()


def sum_scratch(terms):
    rows, width = terms[0][0].shape[0] // 8, terms[0][2].shape[0]
    half, depth, count = rows // 2, sum(term[4] for term in terms), len(terms)
    return [
        pltpu.VMEM((8, rows, depth), jnp.bfloat16),
        pltpu.VMEM((width, depth), jnp.bfloat16),
        pltpu.VMEM((4, rows, width), jnp.bfloat16),
        pltpu.VMEM((4, rows, width), jnp.bfloat16),
        pltpu.VMEM((4, rows, width), jnp.bfloat16),
        pltpu.VMEM((2, half, width), jnp.bfloat16),
        pltpu.VMEM((2, half, width), jnp.bfloat16),
        pltpu.VMEM((half, width), jnp.bfloat16),
        pltpu.VMEM((half, width), jnp.bfloat16),
        pltpu.SemaphoreType.DMA((8, count)),
        pltpu.SemaphoreType.DMA((count,)),
        pltpu.SemaphoreType.DMA((2, 10)),
    ]


def sum_operands(terms):
    return [term[0] for term in terms] + [term[2] for term in terms]


def sum_steps(terms, operands, total, scratch):
    windows = [(term[1], term[3], term[4]) for term in terms]
    return TokenSum(windows, operands[: len(terms)], operands[len(terms) :], total, scratch)


def sum_flops(terms):
    return sum(2 * t[0].shape[0] * t[2].shape[0] * t[4] for t in terms)


def product_sum(terms, number):
    rows, width = terms[0][0].shape[0] // 8, terms[0][2].shape[0]
    count = 2 * len(terms)

    def kernel(*refs):
        steps = sum_steps(terms, refs[:count], refs[count], refs[count + 1 :])
        steps.load()
        greet_partners()
        steps.run(True)
        steps.finish()
        steps.drain()

    return pl.pallas_call(
        kernel,
        in_specs=[pl.BlockSpec(memory_space=pl.ANY)] * count,
        out_specs=pl.BlockSpec(memory_space=pltpu.VMEM),
        out_shape=jax.ShapeDtypeStruct((rows, width), jnp.float32),
        scratch_shapes=sum_scratch(terms),
        compiler_params=pltpu.CompilerParams(collective_id=number, has_side_effects=True),
        cost_estimate=pl.CostEstimate(
            flops=sum_flops(terms), bytes_accessed=100 * rows * width, transcendentals=0
        ),
    )(*sum_operands(terms))


def input_gradient(terms, inputs, gain):
    rows, width = inputs.shape
    count = 2 * len(terms)
    tile = 32

    def kernel(*refs):
        input_ref, gain_ref, grad_out, part_out = refs[count : count + 4]
        steps = sum_steps(terms, refs[:count], grad_out, refs[count + 4 :])
        steps.load()
        greet_partners()
        steps.run(True)
        steps.finish()

        def one_tile(t, part):
            span = pl.ds(pl.multiple_of(t * tile, tile), tile)
            values = input_ref[span, :].astype(jnp.float32)
            inverse = inverse_rms(values)
            normed = values * inverse
            grad_normed = grad_out[span, :]
            scaled = grad_normed * gain_ref[...]
            mean = jnp.mean(scaled * normed, axis=-1, keepdims=True)
            grad_out[span, :] = inverse * (scaled - normed * mean)
            return part + jnp.sum(grad_normed * normed, axis=0, keepdims=True)

        part_out[...] = lax.fori_loop(
            0, rows // tile, one_tile, jnp.zeros((1, width), jnp.float32)
        )
        steps.drain()

    vmem, hbm = pl.BlockSpec(memory_space=pltpu.VMEM), pl.BlockSpec(memory_space=pl.ANY)
    return pl.pallas_call(
        kernel,
        in_specs=[hbm] * count + [vmem] * 2,
        out_specs=[vmem] * 2,
        out_shape=[
            jax.ShapeDtypeStruct((rows, width), jnp.float32),
            jax.ShapeDtypeStruct((1, width), jnp.float32),
        ],
        scratch_shapes=sum_scratch(terms),
        compiler_params=pltpu.CompilerParams(collective_id=6, has_side_effects=True),
        cost_estimate=pl.CostEstimate(
            flops=sum_flops(terms), bytes_accessed=150 * rows * width, transcendentals=rows
        ),
        name="input_gradient",
    )(*sum_operands(terms), inputs, gain.reshape(1, width))


def closing(terms, parts, outer):
    rows, width = terms[0][0].shape[0] // 8, terms[0][2].shape[0]
    count = 2 * len(terms)

    def kernel(*refs):
        part_ref, layer_out, total_out = refs[count : count + 3]
        scratch = refs[count + 3 :]
        held, stages, semaphores, row_semaphores = scratch[-4:]
        output = sum_steps(terms, refs[:count], layer_out, scratch[:-4])
        output.load()
        greet_partners(outer)
        started = []

        def pass_on(step, source):
            copy = send_along(group[step], source, held.at[step], semaphores, step)
            copy.start()
            started.append(copy)

        pass_on(0, part_ref)
        output.run(False)
        value = part_ref[...]
        for step in range(3):
            started[step].wait_recv()
            value = value + held[step]
            stages[step] = value
            if step < 2:
                pass_on(step + 1, stages.at[step])
        for shift in range(1, outer):
            copy = pltpu.make_async_remote_copy(
                src_ref=stages.at[2],
                dst_ref=held.at[2 + shift],
                send_sem=row_semaphores.at[0, shift],
                recv_sem=row_semaphores.at[1, shift],
                device_id=row_partner(shift, outer),
                device_id_type=MESH,
            )
            copy.start()
            started.append(copy)
        output.second()
        output.finish()
        value = stages[2]
        for shift in range(1, outer):
            started[2 + shift].wait_recv()
            value = value + held[2 + shift]
        total_out[...] = value
        for copy in started:
            copy.wait_send()
        output.drain()

    vmem, hbm = pl.BlockSpec(memory_space=pltpu.VMEM), pl.BlockSpec(memory_space=pl.ANY)
    return pl.pallas_call(
        kernel,
        in_specs=[hbm] * count + [vmem],
        out_specs=[vmem] * 2,
        out_shape=[
            jax.ShapeDtypeStruct((rows, width), jnp.float32),
            jax.ShapeDtypeStruct(parts.shape, jnp.float32),
        ],
        scratch_shapes=[
            *sum_scratch(terms),
            pltpu.VMEM((2 + outer, *parts.shape), jnp.float32),
            pltpu.VMEM((3, *parts.shape), jnp.float32),
            pltpu.SemaphoreType.DMA((2, 3)),
            pltpu.SemaphoreType.DMA((2, max(outer, 2))),
        ],
        compiler_params=pltpu.CompilerParams(collective_id=5, has_side_effects=True),
        cost_estimate=pl.CostEstimate(
            flops=sum_flops(terms), bytes_accessed=150 * rows * width, transcendentals=0
        ),
        name="closing",
    )(*sum_operands(terms), parts)


def rope_tables():
    half_dim = HD // 2
    lanes = jnp.arange(PAIR)
    inverse = rope_base ** (-((lanes % half_dim).astype(jnp.float32) * 2.0 / HD))
    angles = jnp.arange(LEN, dtype=jnp.float32)[:, None] * inverse[None, :]
    sign = jnp.where(lanes % HD < half_dim, -1.0, 1.0)
    return jnp.cos(angles), jnp.sin(angles) * sign[None, :]


def turn(values, cosine, signed_sine):
    half_dim = HD // 2
    lanes = lax.broadcasted_iota(jnp.int32, values.shape, 1)
    other = jnp.where(
        lanes % HD < half_dim,
        pltpu.roll(values, PAIR - half_dim, 1),
        pltpu.roll(values, half_dim, 1),
    )
    return values * cosine + other * signed_sine


def head_parts(values):
    lanes = lax.broadcasted_iota(jnp.int32, values.shape, 1)
    empty = jnp.zeros_like(values)
    return [jnp.where(lanes // HD == head, values, empty) for head in range(2)]


def forward_kernel(
    query_ref, key_ref, value_ref, cos_ref, sin_ref, q_out, k_out, v_out, attended_out
):
    cosine, sine = cos_ref[...], sin_ref[...]
    queries = turn(query_ref[...], cosine, sine).astype(jnp.bfloat16)
    keys = turn(key_ref[...], cosine, sine).astype(jnp.bfloat16)
    values = value_ref[...].astype(jnp.bfloat16)
    q_out[...] = queries
    k_out[...] = keys
    v_out[...] = values
    value_parts = head_parts(values)
    scaling = HD**-0.5
    for block in range(LEN // BLK):
        rows = slice(block * BLK, (block + 1) * BLK)
        seen = (block + 1) * BLK
        total = None
        for head, query_part in enumerate(head_parts(queries[rows])):
            scores = contract(query_part, keys[:seen], 1, 1) * scaling
            top = jnp.max(scores, axis=-1, keepdims=True)
            powers = jnp.exp(scores - top)
            weights = powers / jnp.sum(powers, axis=-1, keepdims=True)
            term = contract(weights.astype(jnp.bfloat16), value_parts[head][:seen], 1, 0)
            total = term if total is None else total + term
        attended_out[rows, :] = total.astype(jnp.bfloat16)


def backward_kernel(
    query_ref, key_ref, value_ref, grad_ref, cos_ref, sin_ref, q_out, k_out, v_out, key_acc, value_acc
):
    keys, values = key_ref[...], value_ref[...]
    key_parts = head_parts(keys)
    scaling = HD**-0.5
    key_acc[...] = jnp.zeros_like(key_acc)
    value_acc[...] = jnp.zeros_like(value_acc)
    for block in range(LEN // BLK):
        rows = slice(block * BLK, (block + 1) * BLK)
        seen = (block + 1) * BLK
        query_parts = head_parts(query_ref[rows, :])
        grad_parts = head_parts(grad_ref[rows, :])
        query_delta = None
        for head in range(2):
            scores = contract(query_parts[head], keys[:seen], 1, 1) * scaling
            top = jnp.max(scores, axis=-1, keepdims=True)
            powers = jnp.exp(scores - top)
            weights = powers / jnp.sum(powers, axis=-1, keepdims=True)
            grad_probs = contract(grad_parts[head], values[:seen], 1, 1)
            row_dot = jnp.sum(weights * grad_probs, axis=-1, keepdims=True)
            grad_scores = (weights * (grad_probs - row_dot) * scaling).astype(jnp.bfloat16)
            term = contract(grad_scores, key_parts[head][:seen], 1, 0)
            query_delta = term if query_delta is None else query_delta + term
            key_acc[:seen, :] += contract(grad_scores, query_parts[head], 0, 0)
            value_acc[:seen, :] += contract(weights.astype(jnp.bfloat16), grad_parts[head], 0, 0)
        q_out[rows, :] = turn(query_delta, cos_ref[rows, :], -sin_ref[rows, :]).astype(jnp.bfloat16)
    k_out[...] = turn(key_acc[...], cos_ref[...], -sin_ref[...]).astype(jnp.bfloat16)
    v_out[...] = value_acc[...].astype(jnp.bfloat16)


def attention_cost(rows, width, products):
    return pl.CostEstimate(
        flops=2 * products * rows * LEN * width,
        bytes_accessed=8 * rows * width * 2,
        transcendentals=rows * LEN * width // HD,
    )


def attention_forward(mixed, tables):
    rows, width = mixed.shape[0], mixed.shape[1] // 3
    pairs = width // PAIR

    def part(which):
        return pl.BlockSpec((LEN, PAIR), lambda s, p: (s, which * pairs + p))

    whole = pl.BlockSpec((LEN, PAIR), lambda s, p: (0, 0))
    return pl.pallas_call(
        forward_kernel,
        grid=(rows // LEN, pairs),
        in_specs=[part(0), part(1), part(2), whole, whole],
        out_specs=[part(0)] * 4,
        out_shape=[jax.ShapeDtypeStruct((rows, width), jnp.bfloat16)] * 4,
        cost_estimate=attention_cost(rows, width, 2),
        name="attention_forward",
    )(mixed, mixed, mixed, *tables)


def attention_backward(queries, keys, values, grads, tables):
    rows, width = queries.shape
    part = pl.BlockSpec((LEN, PAIR), lambda s, p: (s, p))
    whole = pl.BlockSpec((LEN, PAIR), lambda s, p: (0, 0))
    return pl.pallas_call(
        backward_kernel,
        grid=(rows // LEN, width // PAIR),
        in_specs=[part] * 4 + [whole] * 2,
        out_specs=[part] * 3,
        out_shape=[jax.ShapeDtypeStruct((rows, width), jnp.bfloat16)] * 3,
        scratch_shapes=[pltpu.VMEM((LEN, PAIR), jnp.float32)] * 2,
        cost_estimate=attention_cost(rows, width, 5),
        name="attention_backward",
    )(queries, keys, values, grads, *tables)


def norm_kernel(input_ref, gain_ref, out_ref):
    values = input_ref[...].astype(jnp.float32)
    out_ref[...] = (values * inverse_rms(values) * gain_ref[...]).astype(jnp.bfloat16)


def norm_rows(inputs, gain):
    rows, width = inputs.shape
    tile = 256
    block = pl.BlockSpec((tile, width), lambda t: (t, 0))
    return pl.pallas_call(
        norm_kernel,
        grid=(rows // tile,),
        in_specs=[block, pl.BlockSpec((1, width), lambda t: (0, 0))],
        out_specs=block,
        out_shape=jax.ShapeDtypeStruct((rows, width), jnp.bfloat16),
        cost_estimate=pl.CostEstimate(
            flops=4 * rows * width, bytes_accessed=4 * rows * width, transcendentals=rows
        ),
        name="norm_rows",
    )(inputs, gain.reshape(1, width))


def product_kernel(left_ref, right_ref, out_ref):
    out_ref[...] = contract(left_ref[...], right_ref[...], 1, 0).astype(out_ref.dtype)


def product(left, right, start, columns, kind):
    rows, width = left.shape
    tile = 512
    return pl.pallas_call(
        product_kernel,
        grid=(rows // tile,),
        in_specs=[
            pl.BlockSpec((tile, width), lambda t: (t, 0)),
            pl.BlockSpec((width, columns), lambda t: (0, start // columns)),
        ],
        out_specs=pl.BlockSpec((tile, columns), lambda t: (t, 0)),
        out_shape=jax.ShapeDtypeStruct((rows, columns), kind),
        cost_estimate=pl.CostEstimate(
            flops=2 * rows * width * columns,
            bytes_accessed=2 * rows * width + 2 * width * columns + 4 * rows * columns,
            transcendentals=0,
        ),
    )(left, right)


def feed_kernel(normed_ref, cotangent_ref, weight_ref, out_ref):
    chunk = out_ref.shape[1] // 3
    gate, up, down = [slice(which * chunk, (which + 1) * chunk) for which in range(3)]
    gate_pre = contract(normed_ref[...], weight_ref[:, gate], 1, 0)
    up_proj = contract(normed_ref[...], weight_ref[:, up], 1, 0)
    grad_act = contract(cotangent_ref[...], weight_ref[:, down], 1, 0)
    sigmoid_gate = jax.nn.sigmoid(gate_pre)
    silu_gate = gate_pre * sigmoid_gate
    gate_slope = sigmoid_gate * (1.0 + gate_pre * (1.0 - sigmoid_gate))
    out_ref[:, gate] = (grad_act * up_proj * gate_slope).astype(jnp.bfloat16)
    out_ref[:, up] = (grad_act * silu_gate).astype(jnp.bfloat16)
    out_ref[:, down] = (silu_gate * up_proj).astype(jnp.bfloat16)


def feed_units(normed, cotangents, weights):
    (rows, width), columns = normed.shape, weights.shape[1]
    tile = 256
    tokens = pl.BlockSpec((tile, width), lambda t: (t, 0))
    return pl.pallas_call(
        feed_kernel,
        grid=(rows // tile,),
        in_specs=[tokens, tokens, pl.BlockSpec((width, columns), lambda t: (0, 0))],
        out_specs=pl.BlockSpec((tile, columns), lambda t: (t, 0)),
        out_shape=jax.ShapeDtypeStruct((rows, columns), jnp.bfloat16),
        cost_estimate=pl.CostEstimate(
            flops=2 * rows * width * columns,
            bytes_accessed=2 * (2 * rows * width + width * columns + rows * columns),
            transcendentals=rows * columns // 3,
        ),
        name="feed_units",
    )(normed, cotangents, weights)


def weight_grads(terms):
    rows, width = terms[0][0].shape
    tile = 256
    operands, specs, plan = [], [], []
    for left, rights in terms:
        operands.append(left)
        specs.append(pl.BlockSpec((rows, tile), lambda t: (0, t)))
        for right, start, columns in rights:
            operands.append(right)
            specs.append(
                pl.BlockSpec((rows, columns), lambda t, block=start // columns: (0, block))
            )
        plan.append([columns for _, _, columns in rights])
    total = sum(sum(widths) for widths in plan)

    def kernel(*refs):
        edge, at = 0, 0
        for widths in plan:
            left = refs[at][...]
            at += 1
            for columns in widths:
                refs[-1][:, edge : edge + columns] = contract(left, refs[at][...], 0, 0).astype(
                    jnp.bfloat16
                )
                edge += columns
                at += 1

    return pl.pallas_call(
        kernel,
        grid=(width // tile,),
        in_specs=specs,
        out_specs=pl.BlockSpec((tile, total), lambda t: (t, 0)),
        out_shape=jax.ShapeDtypeStruct((width, total), jnp.bfloat16),
        cost_estimate=pl.CostEstimate(
            flops=2 * rows * width * total,
            bytes_accessed=2 * (2 * rows * width + width * total + rows * total),
            transcendentals=0,
        ),
    )(*operands)


def own_and_other(weights, first, width):
    side = lax.axis_index("i")

    def columns(half):
        start = [half * (w.shape[1] // 2) + first for w in weights]
        return jnp.concatenate([w[:, a : a + width] for w, a in zip(weights, start)], axis=1)

    low, high = columns(0), columns(1)
    kept = jnp.where(side == 0, low, high)
    return kept, lax.ppermute(jnp.where(side == 0, high, low), "i", swap)


def exchange_rows(weights, first, width):
    return jnp.concatenate(in_order(own_and_other(weights, first, width)))


def row_gather(values):
    return lax.all_gather(values, "o", axis=0, tiled=True)


def row_sum(partial_value):
    return lax.psum_scatter(partial_value, "o", scatter_dimension=0, tiled=True)


def exchange_columns(summed):
    side = lax.axis_index("i")
    rows = summed.shape[0] // 2
    kept = lax.dynamic_slice_in_dim(summed, side * rows, rows, axis=0)
    other = lax.ppermute(
        lax.dynamic_slice_in_dim(summed, (1 - side) * rows, rows, axis=0), "i", swap
    )
    return kept, other


def in_order(halves):
    kept, other = halves
    side = lax.axis_index("i")
    return jnp.where(side == 0, kept, other), jnp.where(side == 0, other, kept)


def inverse_rms(values):
    return lax.rsqrt(jnp.mean(values * values, axis=-1, keepdims=True) + epsilon)


def per_device(
    layer_input,
    query_weight,
    key_weight,
    value_weight,
    out_weight,
    gate_weight,
    up_weight,
    down_weight,
    attention_gain,
    feed_gain,
    out_cotangent,
):
    head_width = query_weight.shape[1] // 2
    hidden = gate_weight.shape[1] // 2
    chunks = [hidden * part // 8 for part in EIGHTHS]
    firsts = [sum(chunks[:k]) for k in range(len(chunks))]
    tables = rope_tables()
    outer = lax.axis_size("o")

    kept, other = own_and_other((query_weight, key_weight, value_weight, out_weight), 0, head_width)
    kept_full = row_gather(kept)
    other_full = row_gather(other)
    feed_full = []
    for first, chunk in zip(firsts, chunks):
        feed_rows = exchange_rows((gate_weight, up_weight, down_weight), first, chunk)
        feed_full.append(row_gather(feed_rows))
    inputs_all, gains = opening_gather(layer_input, jnp.stack([attention_gain, feed_gain]), outer)
    gain_one, gain_two = [g.astype(jnp.float32) for g in gains]
    normed = norm_rows(inputs_all, gain_one)
    normed, tables, late = lax.optimization_barrier((normed, tables, out_cotangent))
    cotangents = token_gather(late)
    inputs = layer_input.astype(jnp.float32)

    blocks = [w.reshape(outer, *kept.shape) for w in (kept_full, other_full)]
    attention_full = jnp.stack(in_order(blocks), axis=1).reshape(-1, kept.shape[1])
    mixed = product(normed, attention_full, 0, 3 * head_width, jnp.float32)
    queries, keys, values, attended = attention_forward(mixed, tables)
    hidden_state = inputs + product_sum(
        [(attended, 0, attention_full, 3 * head_width, head_width)], 3
    )
    inv_two = inverse_rms(hidden_state)
    normed_two_raw = hidden_state * inv_two
    normed_two = token_gather((normed_two_raw * gain_two).astype(jnp.bfloat16))

    output_terms, grad_terms, feed_grads = [], [], []
    for k, chunk in enumerate(chunks):
        units = feed_units(normed_two, cotangents, feed_full[k])
        grads = weight_grads(
            [
                (normed_two, [(units, 0, 2 * chunk)]),
                (cotangents, [(units, 2 * chunk, chunk)]),
            ],
        )
        units, grads, normed_two, cotangents = lax.optimization_barrier(
            (units, grads, normed_two, cotangents)
        )
        summed = row_sum(grads)
        feed_grads.append(exchange_columns(summed))
        grad_terms.append((units, 0, feed_full[k], 0, 2 * chunk))
        output_terms.append((units, 2 * chunk, feed_full[k], 2 * chunk, chunk))

    grad_normed_two = product_sum(grad_terms, 4)
    feed_gain_part = jnp.sum(grad_normed_two * normed_two_raw, axis=0, keepdims=True)
    scaled_two = grad_normed_two * gain_two
    grad_hidden = out_cotangent.astype(jnp.float32) + inv_two * (
        scaled_two - normed_two_raw * jnp.mean(scaled_two * normed_two_raw, axis=-1, keepdims=True)
    )
    grad_rows = token_gather(grad_hidden.astype(jnp.bfloat16))
    grad_attended = product(grad_rows, attention_full, 3 * head_width, head_width, jnp.bfloat16)
    grad_query, grad_key, grad_value = attention_backward(
        queries, keys, values, grad_attended, tables
    )
    attention_grads = weight_grads(
        [
            (normed, [(g, 0, head_width) for g in (grad_query, grad_key, grad_value)]),
            (grad_rows, [(attended, 0, head_width)]),
        ],
    )
    attention_grads, grad_query = lax.optimization_barrier((attention_grads, grad_query))
    attention_summed = row_sum(attention_grads)
    attention_halves = exchange_columns(attention_summed)
    norm_grad, attention_gain_part = input_gradient(
        [
            (g, 0, attention_full, which * head_width, head_width)
            for which, g in enumerate((grad_query, grad_key, grad_value))
        ],
        layer_input,
        gain_one,
    )
    parts = jnp.concatenate([attention_gain_part, feed_gain_part, jnp.zeros((6, feed_gain_part.shape[1]))])
    feed_output, gain_sums = closing(output_terms, parts, outer)

    def whole_rows(halves, which, widths):
        return jnp.concatenate(
            [
                part[:, which * width : (which + 1) * width]
                for half in zip(*halves)
                for part, width in zip(half, widths)
            ],
            axis=1,
        ).astype(jnp.float32)

    input_grad = grad_hidden + norm_grad
    layer_output = hidden_state + feed_output
    feed_halves = [in_order(halves) for halves in feed_grads]
    feed_rows = [whole_rows(feed_halves, which, chunks) for which in range(3)]
    attention_halves = [in_order(attention_halves)]
    attention_rows = [whole_rows(attention_halves, which, [head_width]) for which in range(4)]
    device = lax.axis_index("o")
    for axis in group:
        device = device * 2 + lax.axis_index(axis)
    share = attention_gain.shape[0] // 4
    gain_grads = [
        lax.dynamic_slice_in_dim(gain_sums[which], device * share, share) for which in range(2)
    ]
    return (
        layer_output,
        input_grad,
        *attention_rows,
        *feed_rows,
        *gain_grads,
    )


def solution(mesh):
    rows, columns = mesh.shape["dp"], mesh.shape["tensor"]
    fine = Mesh(
        mesh.devices.reshape(rows // 2, 2, columns // 2, 2), ("o", "i", "y", "c")
    )
    tokens = P(("o", "i", "y", "c"), None)
    weight = P(("o", "i"), ("y", "c"))
    gain = P(("o", "i"))

    return jax.shard_map(
        per_device,
        mesh=fine,
        in_specs=(tokens, *[weight] * 7, gain, gain, tokens),
        out_specs=(tokens, tokens, *[weight] * 7, P(("o", "i", "y", "c")), P(("o", "i", "y", "c"))),
        check_vma=False,
    )
```
